128 devices in a mesh: slab: 16 (over x, y_hi, core), tile: 8 (over y_lo, z).
Axes of the slice: x: 4, y: 4 (y_hi: 2, y_lo: 2; y = y_hi * 2 + y_lo), z: 4, core: 2. Of those that a mesh axis runs over, the one named last changes fastest.
Arguments:
- velocity: float32 [3, 512, 128, 128], P(None, 'slab', 'tile'), may hold values from -4 to 4
- viscosity: float32 [512, 128, 128], P('slab', 'tile'), may hold values from 0.2 to 0.6
- basis: bfloat16 [32, 3, 512, 128, 128], P(None, None, ('slab', 'tile')), may hold values from -6 to 6
- sigma: float32 [32], replicated, may hold values from 0.3 to 3
- rotation: float32 [35, 32], replicated, may hold values from -1 to 1
Outputs:
- advanced: float32 [3, 512, 128, 128], P(None, 'slab', 'tile')
- r_factor: float32 [35, 35], replicated
- new_basis: bfloat16 [32, 3, 512, 128, 128], P(None, None, ('slab', 'tile'))
The draws below stay inside these ranges and needn't reach their ends.
All inputs are finite; a program needn't handle non-finite values.
Results may differ from the reference program's by a relative error of at most 0.001.
Values sent between devices are 32-bit elements; how exact they have to be, the bound alone decides.
A program may use at most 256 MiB of HBM per device.

```python
import math
import jax
import jax.numpy as jnp
from jax import lax

NY = 128
RANK = 32
K = 35
NX = 512
NZ = 128
N_SLAB = 16
N_TILE = 8


def flow_draw(key):
    field_key = jax.random.fold_in(key, 7001)
    velocity_draw = jnp.clip(jax.random.normal(field_key, (3, NX, NZ, NY), jnp.float32), -4.0, 4.0)
    return velocity_draw


def draw_velocity(key, part):
    return flow_draw(key)


def draw_basis(key, part):
    shared_count = 4
    flow_values = flow_draw(key)
    own_key, common_key, weight_key, along_key = jax.random.split(jax.random.fold_in(key, 7002), 4)
    own_part = jax.random.normal(own_key, (RANK, 3, NX, NZ, NY), jnp.float32)
    common = jax.random.normal(common_key, (shared_count, 3, NX, NZ, NY), jnp.float32)
    weights = jax.random.uniform(weight_key, (RANK, shared_count), jnp.float32, -0.6, 0.6)
    along_flow = jax.random.uniform(along_key, (RANK,), jnp.float32, -0.8, 0.8)
    mixture = own_part + along_flow[:, None, None, None, None] * flow_values[None]
    for member in range(shared_count):
        mixture = mixture + weights[:, member][:, None, None, None, None] * common[member][None]
    return jnp.clip(mixture, -6.0, 6.0).astype(jnp.bfloat16)


def levels(key, dims, shards, smallest, high):
    gain, own = 1.0, jax.random.fold_in(key, 6)
    for axis_at, parts in shards:
        steps = jnp.exp(jax.random.uniform(jax.random.fold_in(own, axis_at), (parts,), jnp.float32, smallest / len(shards), high / len(shards)))
        gain = gain * jnp.repeat(steps, dims[axis_at] // parts).reshape([-1 if axis == axis_at else 1 for axis in range(len(dims))])
    return gain


def gaussian(key, extent, spread, limit, kind=jnp.bfloat16):
    return jnp.clip(spread * jax.random.normal(key, extent, jnp.float32), -limit, limit).astype(kind)


def setup_inputs(seed: int = 0) -> dict:
    splits = jax.random.split(jax.random.key(seed), 6)
    velocity = draw_velocity(jax.random.fold_in(splits[5], 71), 0)
    viscosity = jnp.clip(jnp.exp(math.log(0.6) - 1.0986123 * jax.random.uniform(splits[1], (NX, NZ, NY), jnp.float32) ** levels(splits[1], (NX, NZ, NY), ((0, 16), (1, 8)), -0.2, 0.2)), 0.2, 0.6)
    basis = draw_basis(jax.random.fold_in(splits[5], 71), 0)
    sigma = jnp.clip(jnp.exp(jax.random.uniform(splits[3], (RANK,), jnp.float32, math.log(0.3), math.log(3.0))), 0.3, 3.0)
    rotation = gaussian(splits[4], (K, RANK), K ** -0.5, 1.0, jnp.float32)
    return {"velocity": velocity, "viscosity": viscosity, "basis": basis, "sigma": sigma, "rotation": rotation}


step_size = 0.25

def upper_factor(gram):
    order = gram.shape[0]
    positions = jnp.arange(order)
    factor = jnp.zeros_like(gram)
    for column_index in range(order):
        above = factor[:, column_index]
        remainder = gram[column_index] - jnp.dot(above, factor, precision=lax.Precision.HIGHEST, preferred_element_type=jnp.float32)
        pivot = jnp.sqrt(remainder[column_index])
        new_row = jnp.where(positions >= column_index, remainder / pivot, 0.0)
        factor = factor.at[column_index].set(new_row)
    return factor

def upper_solve(factor, right_hand):
    order = factor.shape[0]
    solved = jnp.zeros_like(right_hand)
    for row_index in range(order - 1, -1, -1):
        partial_sum = jnp.dot(factor[row_index], solved, precision=lax.Precision.HIGHEST, preferred_element_type=jnp.float32)
        solved = solved.at[row_index].set((right_hand[row_index] - partial_sum) / factor[row_index, row_index])
    return solved

def wrap_pad(flow_state, margin):
    return jnp.pad(flow_state, ((0, 0), (margin, margin), (margin, margin), (0, 0)), mode='wrap')

def advance(padded, viscosity):
    centre = padded[:, 1:-1, 1:-1, :]
    forward_x = padded[:, 2:, 1:-1, :]
    backward_x = padded[:, :-2, 1:-1, :]
    forward_z = padded[:, 1:-1, 2:, :]
    backward_z = padded[:, 1:-1, :-2, :]
    walled = jnp.pad(centre, ((0, 0), (0, 0), (0, 0), (1, 1)))
    above_y = walled[..., 2:]
    below_y = walled[..., :-2]
    laplace = forward_x + backward_x + forward_z + backward_z + above_y + below_y - 6.0 * centre
    carried = centre[0:1] * (forward_x - backward_x) + centre[1:2] * (above_y - below_y) + centre[2:3] * (forward_z - backward_z)
    return centre + step_size * (viscosity * laplace - 0.5 * carried)

def reference(velocity, viscosity, basis, sigma, rotation):
    first_step = advance(wrap_pad(velocity, 1), viscosity)
    advanced = advance(wrap_pad(first_step, 1), viscosity)
    snapshots = jnp.stack([velocity, first_step, advanced])
    block_count = N_SLAB * N_TILE
    block_width = NX // block_count
    width_all = RANK + 3

    def block_columns(block_index):
        block_start = (block_index * block_width).astype(jnp.int32)
        basis_part = lax.dynamic_slice_in_dim(basis, block_start, block_width, 2).astype(jnp.float32)
        basis_part = basis_part * sigma[:, None, None, None, None]
        snap_part = lax.dynamic_slice_in_dim(snapshots, block_start, block_width, 2)
        return jnp.concatenate([basis_part, snap_part], 0).reshape(width_all, -1)

    def add_block(block_index, running):
        columns = block_columns(block_index)
        return running + jnp.dot(columns, columns.T, precision=lax.Precision.HIGHEST, preferred_element_type=jnp.float32)
    gram = lax.fori_loop(0, block_count, add_block, jnp.zeros((width_all, width_all), jnp.float32))
    factor = upper_factor(gram)
    row_scale = math.sqrt(3 * NX * NZ * NY)
    mixing = upper_solve(factor, rotation) * row_scale

    def write_block(block_index, assembled):
        columns = block_columns(block_index)
        new_piece = jnp.dot(mixing.T, columns, precision=lax.Precision.HIGHEST, preferred_element_type=jnp.float32)
        new_piece = new_piece.reshape(RANK, 3, block_width, NZ, NY).astype(jnp.bfloat16)
        block_start = (block_index * block_width).astype(jnp.int32)
        return lax.dynamic_update_slice_in_dim(assembled, new_piece, block_start, 2)
    new_basis = lax.fori_loop(0, block_count, write_block, jnp.zeros((RANK, 3, NX, NZ, NY), jnp.bfloat16))
    return (advanced, factor / row_scale, new_basis)
```

```python
import functools
import math

import jax
import jax.numpy as jnp
from jax import lax
from jax.experimental import pallas as pl
from jax.experimental.pallas import tpu as pltpu
from jax.sharding import PartitionSpec as P

step_size = 0.25
RANK = 32
SNAPS = 3
K = RANK + SNAPS
SUB = 8
LANES = 128
WIDE = RANK * SUB
F32 = jnp.float32
BF16 = jnp.bfloat16
HIGHEST = lax.Precision.HIGHEST


def iota(shape, dim):
    return lax.broadcasted_iota(jnp.int32, shape, dim)


def extended(block, sides, width):
    for axis, dim in sides:
        count = lax.axis_size(axis)
        forward = [(i, i + 1) for i in range(count - 1)]
        forward.append((count - 1, 0))
        backward = [(target, source) for source, target in forward]
        low = lax.ppermute(
            lax.slice_in_dim(block, block.shape[dim] - width, None, axis=dim), axis, forward
        )
        high = lax.ppermute(lax.slice_in_dim(block, 0, width, axis=dim), axis, backward)
        block = jnp.concatenate([low, block, high], axis=dim)
    return block


def advance(padded, viscosity):
    centre = padded[:, 1:-1, 1:-1, :]
    forward_x = padded[:, 2:, 1:-1, :]
    backward_x = padded[:, :-2, 1:-1, :]
    forward_z = padded[:, 1:-1, 2:, :]
    backward_z = padded[:, 1:-1, :-2, :]
    walled = jnp.pad(centre, ((0, 0), (0, 0), (0, 0), (1, 1)))
    above_y = walled[..., 2:]
    below_y = walled[..., :-2]
    laplace = forward_x + backward_x + forward_z + backward_z + above_y + below_y - 6.0 * centre
    carried = (
        centre[0:1] * (forward_x - backward_x)
        + centre[1:2] * (above_y - below_y)
        + centre[2:3] * (forward_z - backward_z)
    )
    return centre + step_size * (viscosity * laplace - 0.5 * carried)


def pieces(values, count):
    parts = []
    for _ in range(count):
        part = values.astype(BF16)
        parts.append(part)
        values = values - part.astype(F32)
    return parts


def matched(product, rows):
    same = iota(product.shape, 0) % SUB == iota(product.shape, 1) % SUB
    summed = jnp.where(same, product, 0.0).reshape(rows, SUB, WIDE).sum(1)
    pick = (iota((WIDE, LANES), 0) // SUB == iota((WIDE, LANES), 1)).astype(F32)
    return jnp.dot(summed, pick, precision=HIGHEST, preferred_element_type=F32)


def basis_columns(x_ref):
    tiles = x_ref.shape[2]
    return jnp.concatenate([x_ref[:, 0, t].reshape(WIDE, LANES) for t in range(tiles)], axis=1)


def basis_gram_kernel(x_ref, out_ref, total):
    step = pl.program_id(0)

    @pl.when(step == 0)
    def _():
        total[...] = jnp.zeros_like(total)

    columns = basis_columns(x_ref)
    total[...] += lax.dot_general(
        columns, columns, (((1,), (1,)), ((), ())), preferred_element_type=F32
    )

    @pl.when(step == pl.num_programs(0) - 1)
    def _():
        out_ref[...] = matched(total[...], RANK)


def snap_gram_kernel(s_ref, x_ref, out_ref, total, squares):
    step = pl.program_id(0)
    tiles = s_ref.shape[2]

    @pl.when(step == 0)
    def _():
        total[...] = jnp.zeros_like(total)
        squares[...] = jnp.zeros_like(squares)

    rows = []
    for s in range(SNAPS):
        flat = jnp.concatenate([s_ref[s, 0, t] for t in range(tiles)], axis=1)
        rows.extend(pieces(flat, 3))
    rows = jnp.concatenate(rows, axis=0)
    total[...] += lax.dot_general(
        rows, basis_columns(x_ref), (((1,), (1,)), ((), ())), preferred_element_type=F32
    )
    for a in range(SNAPS):
        for b in range(a + 1):
            squares[3 * a + b] += (s_ref[a, 0] * s_ref[b, 0]).sum(0)

    @pl.when(step == pl.num_programs(0) - 1)
    def _():
        by_part = matched(total[...], 3 * SNAPS)
        row = iota((SUB, LANES), 0)
        lane = iota((SUB, LANES), 1)
        result = jnp.zeros((SUB, LANES), F32)
        for s in range(SNAPS):
            line = by_part[3 * s : 3 * s + 1] + by_part[3 * s + 1 : 3 * s + 2] + by_part[3 * s + 2 : 3 * s + 3]
            result = jnp.where(row == s, line, result)
        for a in range(SNAPS):
            for b in range(a + 1):
                value = jnp.sum(squares[3 * a + b])
                result = jnp.where((row == a) & (lane == RANK + b), value, result)
        out_ref[...] = result


def mix_kernel(row_scale, gb_ref, gs_ref, sigma_ref, rotation_ref, factor_ref, weight_ref, snap_ref):
    rows = 40
    row = iota((rows, LANES), 0)
    lane = iota((rows, LANES), 1)
    low = jnp.concatenate([gb_ref[...], gs_ref[...]], axis=0)
    weight = jnp.where(iota((1, LANES), 1) < RANK, sigma_ref[...], 1.0)
    wide_weight = jnp.broadcast_to(weight, (LANES, LANES))
    low = low * weight * wide_weight.T[:rows]
    high = jnp.concatenate([low, jnp.zeros((LANES - rows, LANES), F32)], axis=0).T[:rows]
    gram = jnp.where((row < RANK) & (lane >= RANK), high, low)
    upper_right = (row >= RANK) & (lane > row)
    gram = jnp.where(upper_right, high, gram)
    gram = jnp.where((lane < K) & (row < K), gram, 0.0)
    start = gram + jnp.where((lane == row + 64) | ((lane == row) & (row >= K)), 1.0, 0.0)
    blocks = [start[SUB * b : SUB * b + SUB] for b in range(rows // SUB)]
    sub = iota((SUB, LANES), 0)
    for i in range(K):
        at, inner = divmod(i, SUB)
        pivot_row = blocks[at][inner : inner + 1, :]
        scaled = pivot_row / pivot_row[:, i : i + 1]
        for b in range(at, rows // SUB):
            column = blocks[b][:, i : i + 1]
            update = column * scaled
            if b == at:
                update = jnp.where(sub > inner, update, 0.0)
            blocks[b] = blocks[b] - update
    done = jnp.concatenate(blocks, axis=0)
    pivots = jnp.sum(jnp.where(lane == row, done, 0.0), axis=1, keepdims=True)
    done = done / jnp.sqrt(pivots)
    factor = jnp.where(lane >= row, done, 0.0) * (1.0 / row_scale)
    factor_ref[...] = factor[:K, :K]
    inverse = jnp.where(row < K, done, 0.0)
    mixed = row_scale * lax.dot_general(
        rotation_ref[...],
        inverse,
        (((0,), (0,)), ((), ())),
        precision=HIGHEST,
        preferred_element_type=F32,
    )
    mixed = mixed[:RANK]
    sigma_lane = jnp.concatenate([jnp.zeros((1, 64), F32), sigma_ref[:, :64]], axis=1)
    spread = ((iota((LANES, WIDE), 0) - 64) == iota((LANES, WIDE), 1) // SUB).astype(BF16)
    same = iota((WIDE, WIDE), 0) % SUB == iota((WIDE, WIDE), 1) % SUB
    for part, values in enumerate(pieces(mixed * sigma_lane, 2)):
        wide = jnp.dot(values, spread, preferred_element_type=F32)
        tall = jnp.broadcast_to(wide[:, None, :], (RANK, SUB, WIDE)).reshape(WIDE, WIDE)
        weight_ref[WIDE * part : WIDE * part + WIDE] = jnp.where(same, tall, 0.0).astype(BF16)
    for s in range(SNAPS):
        column = mixed[:, 64 + RANK + s : 64 + RANK + s + 1]
        snap_ref[s] = jnp.broadcast_to(column[:, :, None], (RANK, SUB, LANES))


def apply_kernel(w_ref, c_ref, s_ref, x_ref, o_ref):
    tiles = x_ref.shape[2]
    for t in range(0, tiles, 2):
        pair = jnp.concatenate(
            [x_ref[:, 0, t].reshape(WIDE, LANES), x_ref[:, 0, t + 1].reshape(WIDE, LANES)], axis=1
        )
        both = jnp.dot(w_ref[...], pair, preferred_element_type=F32)
        both = both[:WIDE] + both[WIDE:]
        for half in range(2):
            value = both[:, LANES * half : LANES * half + LANES].reshape(RANK, SUB, LANES)
            for s in range(SNAPS):
                value = value + c_ref[s] * s_ref[s, 0, t + half][None]
            o_ref[:, 0, t + half] = value.astype(BF16)


params = pltpu.CompilerParams(vmem_limit_bytes=60 << 20)


def cost(flops, moved):
    return pl.CostEstimate(flops=flops, bytes_accessed=moved, transcendentals=0)


def shards(velocity, viscosity, basis, sigma, rotation):
    current = velocity
    history = [velocity]
    for repeat in range(2):
        padded = extended(current, (("slab", 1), ("tile", 2)), 1)
        current = advance(padded, viscosity)
        history.append(current)
    snapshots = lax.all_to_all(jnp.stack(history), "tile", split_axis=2, concat_axis=3, tiled=True)
    _, parts, width, deep, lanes = basis.shape
    planes, tiles = parts * width, deep // SUB
    row_count = planes * deep * lanes * lax.axis_size("slab") * lax.axis_size("tile")
    row_scale = math.sqrt(row_count)
    modes = basis.reshape(RANK, planes, tiles, SUB, LANES)
    snaps = snapshots.reshape(SNAPS, planes, tiles, SUB, LANES)
    mode_spec = pl.BlockSpec((RANK, 1, tiles, SUB, LANES), lambda i: (0, i, 0, 0, 0))
    snap_spec = pl.BlockSpec((SNAPS, 1, tiles, SUB, LANES), lambda i: (0, i, 0, 0, 0))
    basis_gram = pl.pallas_call(
        basis_gram_kernel,
        grid=(planes,),
        in_specs=[mode_spec],
        out_specs=pl.BlockSpec((RANK, LANES), lambda i: (0, 0)),
        out_shape=jax.ShapeDtypeStruct((RANK, LANES), F32),
        scratch_shapes=[pltpu.VMEM((WIDE, WIDE), F32)],
        compiler_params=params,
        cost_estimate=cost(6_000_000_000, 12_600_000),
        name="basis_gram",
    )(modes)
    snap_gram = pl.pallas_call(
        snap_gram_kernel,
        grid=(planes,),
        in_specs=[snap_spec, mode_spec],
        out_specs=pl.BlockSpec((SUB, LANES), lambda i: (0, 0)),
        out_shape=jax.ShapeDtypeStruct((SUB, LANES), F32),
        scratch_shapes=[
            pltpu.VMEM((3 * SNAPS * SUB, WIDE), F32),
            pltpu.VMEM((9, SUB, LANES), F32),
        ],
        compiler_params=params,
        cost_estimate=cost(6_000_000_000, 15_000_000),
        name="snap_gram",
    )(snaps, modes)
    whole = lax.psum(jnp.concatenate([basis_gram, snap_gram], axis=0), ("slab", "tile"))
    sigma_row = jnp.pad(sigma[None], ((0, 0), (0, LANES - RANK)))
    rotation_wide = jnp.pad(rotation, ((0, 40 - K), (0, LANES - RANK)))
    factor, weight, snap_weight = pl.pallas_call(
        functools.partial(mix_kernel, row_scale),
        out_shape=(
            jax.ShapeDtypeStruct((K, K), F32),
            jax.ShapeDtypeStruct((2 * WIDE, WIDE), BF16),
            jax.ShapeDtypeStruct((SNAPS, RANK, SUB, LANES), F32),
        ),
        compiler_params=params,
        name="mix",
    )(whole[:RANK], whole[RANK:], sigma_row, rotation_wide)
    rotated = pl.pallas_call(
        apply_kernel,
        grid=(planes,),
        in_specs=[
            pl.BlockSpec((2 * WIDE, WIDE), lambda i: (0, 0)),
            pl.BlockSpec((SNAPS, RANK, SUB, LANES), lambda i: (0, 0, 0, 0)),
            snap_spec,
            mode_spec,
        ],
        out_specs=mode_spec,
        out_shape=jax.ShapeDtypeStruct(modes.shape, BF16),
        compiler_params=params,
        cost_estimate=cost(12_000_000_000, 27_000_000),
        name="apply",
    )(weight, snap_weight, snaps, modes)
    return (current, factor, rotated.reshape(basis.shape))


def solution(mesh):
    in_specs = (
        P(None, "slab", "tile", None),
        P("slab", "tile", None),
        P(None, None, ("slab", "tile"), None, None),
        P(),
        P(),
    )
    out_specs = (P(None, "slab", "tile", None), P(), P(None, None, ("slab", "tile"), None, None))
    return jax.shard_map(shards, mesh=mesh, in_specs=in_specs, out_specs=out_specs, check_vma=False)
```

```python
import functools
import math

import jax
import jax.numpy as jnp
from jax import lax
from jax.experimental import pallas as pl
from jax.experimental.pallas import tpu as pltpu
from jax.sharding import PartitionSpec as P

step_size = 0.25
RANK = 32
SNAPS = 3
K = RANK + SNAPS
SUB = 8
LANES = 128
WIDE = RANK * SUB
F32 = jnp.float32
BF16 = jnp.bfloat16
HIGHEST = lax.Precision.HIGHEST
MESH = pl.DeviceIdType.MESH
GRAM_ROWS = 40
EXCHANGE_VMEM = 63_700_000
ROTATE_VMEM = 50 << 20


def iota(shape, dim):
    return lax.broadcasted_iota(jnp.int32, shape, dim)


def pieces(values, count):
    parts = []
    for _ in range(count):
        part = values.astype(BF16)
        parts.append(part)
        values = values - part.astype(F32)
    return parts


def matched(product, rows):
    same = iota(product.shape, 0) % SUB == iota(product.shape, 1) % SUB
    summed = jnp.where(same, product, 0.0).reshape(rows, SUB, WIDE).sum(1)
    pick = (iota((WIDE, LANES), 0) // SUB == iota((WIDE, LANES), 1)).astype(F32)
    return jnp.dot(summed, pick, precision=HIGHEST, preferred_element_type=F32)


def wide_pair(ref, *index):
    *front, tile = index
    left = ref[(slice(None), *front, tile)].reshape(WIDE, LANES)
    right = ref[(slice(None), *front, tile + 1)].reshape(WIDE, LANES)
    return jnp.concatenate([left, right], axis=1)


def advance_planes(padded, low, high, viscosity, store):
    count = viscosity.shape[0]
    depth = 2 * SUB
    row = iota((depth, LANES), 0)
    lane = iota((depth, LANES), 1)

    def plane(x, carry):
        def at(c, p):
            return padded[c, p].reshape(depth, LANES)

        flow = [at(c, x + 1) for c in range(3)]
        nu = viscosity[x].reshape(depth, LANES)
        for c in range(3):
            centre = flow[c]
            forward_x, backward_x = at(c, x + 2), at(c, x)
            forward_z = jnp.where(row == depth - 1, high[c, pl.ds(x, 1)], pltpu.roll(centre, depth - 1, 0))
            backward_z = jnp.where(row == 0, low[c, pl.ds(x, 1)], pltpu.roll(centre, 1, 0))
            above_y = jnp.where(lane == LANES - 1, 0.0, pltpu.roll(centre, LANES - 1, 1))
            below_y = jnp.where(lane == 0, 0.0, pltpu.roll(centre, 1, 1))
            laplace = forward_x + backward_x + forward_z + backward_z + above_y + below_y - 6.0 * centre
            carried = (
                flow[0] * (forward_x - backward_x)
                + flow[1] * (above_y - below_y)
                + flow[2] * (forward_z - backward_z)
            )
            store(c, x, centre + step_size * (nu * laplace - 0.5 * carried))
        return carry

    lax.fori_loop(0, count, plane, 0)


def exchange_kernel(
    slabs,
    tiles,
    vel_hbm,
    nu_hbm,
    modes_hbm,
    advanced,
    gram_ref,
    snaps,
    modes,
    flow,
    nu,
    low,
    high,
    low_edge,
    high_edge,
    products,
    squares,
    sums_one,
    sums_two,
    late_sums_one,
    late_sums_two,
    load_sem,
    mode_sem,
    own_sem,
    face_send,
    face_recv,
    bulk_send,
    bulk_recv,
    one_send,
    one_recv,
    two_send,
    two_recv,
):
    slab, tile = lax.axis_index("slab"), lax.axis_index("tile")
    planes = modes.shape[1]
    width = snaps.shape[2]
    count = nu.shape[0]

    def shifted(index, by, size):
        return lax.rem(index + by + size, size)

    loads = [
        pltpu.make_async_copy(vel_hbm, flow.at[0, :, 1 : count + 1], load_sem.at[0]),
        pltpu.make_async_copy(nu_hbm, nu, load_sem.at[1]),
    ]
    for copy in loads:
        copy.start()

    barrier = pltpu.get_barrier_semaphore()
    for d in range(1, tiles):
        pl.semaphore_signal(barrier, inc=1, device_id={"tile": shifted(tile, d, tiles)}, device_id_type=MESH)
    for d in range(1, slabs):
        pl.semaphore_signal(barrier, inc=1, device_id={"slab": shifted(slab, d, slabs)}, device_id_type=MESH)

    def mode_copy(plane):
        return pltpu.make_async_copy(modes_hbm.at[:, plane], modes.at[:, plane], mode_sem.at[plane])

    for copy in loads:
        copy.wait()
    for plane in range(planes):
        mode_copy(plane).start()

    def edges(x, carry):
        for c in range(3):
            low_edge[0, c, pl.ds(x, 1)] = flow[0, c, x + 1, 0, 0:1]
            high_edge[0, c, pl.ds(x, 1)] = flow[0, c, x + 1, 1, SUB - 1 : SUB]
        return carry

    lax.fori_loop(0, count, edges, 0)
    pl.semaphore_wait(barrier, tiles + slabs - 2)

    def faces(step):
        up_x, down_x = {"slab": shifted(slab, 1, slabs)}, {"slab": shifted(slab, -1, slabs)}
        up_z, down_z = {"tile": shifted(tile, 1, tiles)}, {"tile": shifted(tile, -1, tiles)}
        moves = [
            (low_edge.at[step], high.at[step], down_z),
            (high_edge.at[step], low.at[step], up_z),
            (flow.at[step, :, count], flow.at[step, :, 0], up_x),
            (flow.at[step, :, 1], flow.at[step, :, count + 1], down_x),
        ]
        return [
            pltpu.make_async_remote_copy(
                src_ref=source,
                dst_ref=target,
                send_sem=face_send.at[step, i],
                recv_sem=face_recv.at[step, i],
                device_id=device,
                device_id_type=MESH,
            )
            for i, (source, target, device) in enumerate(moves)
        ]

    def strip(k, owner):
        start = owner * width
        if k == 2:
            return advanced.at[:, pl.ds(start, width)]
        return flow.at[k, :, pl.ds(start + 1, width)]

    def bulk(k, d):
        owner = shifted(tile, d, tiles)
        return pltpu.make_async_remote_copy(
            src_ref=strip(k, owner),
            dst_ref=snaps.at[k, :, :, pl.ds(2 * tile, 2)],
            send_sem=bulk_send.at[k, d],
            recv_sem=bulk_recv.at[k, d],
            device_id={"tile": owner},
            device_id_type=MESH,
        )

    def own(k):
        return pltpu.make_async_copy(strip(k, tile), snaps.at[k, :, :, pl.ds(2 * tile, 2)], own_sem.at[k])

    def send_strips(k):
        for d in range(1, tiles):
            bulk(k, d).start()
        own(k).start()

    def gram_planes(first, last):
        def plane_step(plane, carry):
            mode_copy(plane).wait()
            columns = jnp.concatenate(
                [wide_pair(modes, plane, t) for t in range(0, modes.shape[2], 2)], axis=1
            )
            products[...] += lax.dot_general(
                columns, columns, (((1,), (1,)), ((), ())), preferred_element_type=F32
            )
            return carry

        lax.fori_loop(first, last, plane_step, 0)

    first_faces = faces(0)
    for copy in first_faces:
        copy.start()
    send_strips(0)
    products[...] = jnp.zeros_like(products)
    squares[...] = jnp.zeros_like(squares)
    gram_planes(0, planes // 2)
    for copy in first_faces:
        copy.wait()

    def store_first(c, x, value):
        flow[1, c, x + 1] = value.reshape(2, SUB, LANES)
        low_edge[1, c, pl.ds(x, 1)] = value[0:1]
        high_edge[1, c, pl.ds(x, 1)] = value[2 * SUB - 1 :]

    advance_planes(flow.at[0], low.at[0], high.at[0], nu, store_first)
    second_faces = faces(1)
    for copy in second_faces:
        copy.start()
    send_strips(1)
    gram_planes(planes // 2, planes)
    for copy in second_faces:
        copy.wait()

    def store_second(c, x, value):
        advanced[c, x] = value.reshape(2, SUB, LANES)

    advance_planes(flow.at[1], low.at[1], high.at[1], nu, store_second)
    send_strips(2)

    def reduce_start(axis, size, sums, send, recv):
        me = lax.axis_index(axis)
        return [
            pltpu.make_async_remote_copy(
                src_ref=sums.at[0],
                dst_ref=sums.at[1 + me],
                send_sem=send.at[d],
                recv_sem=recv.at[d],
                device_id={axis: shifted(me, d, size)},
                device_id_type=MESH,
            )
            for d in range(1, size)
        ]

    def reduce_end(axis, size, sums, copies):
        me = lax.axis_index(axis)
        sums[1 + me] = sums[0]
        for copy in copies:
            copy.wait()
        total = sums[1]
        for i in range(1, size):
            total = total + sums[1 + i]
        return total

    sums_one[0] = matched(products[...], RANK)
    basis_one = reduce_start("tile", tiles, sums_one, one_send.at[0], one_recv.at[0])
    for copy in basis_one:
        copy.start()

    snap_rows = 3 * SNAPS * SUB
    products[:snap_rows] = jnp.zeros((snap_rows, WIDE), F32)

    def piece(d, carry):
        @pl.when(d == 0)
        def _():
            for k in range(SNAPS):
                own(k).wait()

        @pl.when(d > 0)
        def _():
            for k in range(SNAPS):
                bulk(k, d).wait_recv()

        at = 2 * shifted(tile, -d, tiles)
        columns = jnp.concatenate([wide_pair(modes, p, at) for p in range(planes)], axis=1)
        rows = []
        for k in range(SNAPS):
            flat = jnp.concatenate(
                [
                    snaps[k, p // width, p % width, at + h]
                    for p in range(planes)
                    for h in range(2)
                ],
                axis=1,
            )
            rows.extend(pieces(flat, 3))
        products[:snap_rows] += lax.dot_general(
            jnp.concatenate(rows, axis=0),
            columns,
            (((1,), (1,)), ((), ())),
            preferred_element_type=F32,
        )
        for a in range(SNAPS):
            for b in range(a + 1):
                total = jnp.zeros((SUB, LANES), F32)
                for p in range(planes):
                    for h in range(2):
                        c, w = divmod(p, width)
                        total = total + snaps[a, c, w, at + h] * snaps[b, c, w, at + h]
                squares[3 * a + b] += total
        return carry

    lax.fori_loop(0, tiles // 2, piece, 0)
    sums_two[0] = reduce_end("tile", tiles, sums_one, basis_one)
    basis_two = reduce_start("slab", slabs, sums_two, two_send.at[0], two_recv.at[0])
    for copy in basis_two:
        copy.start()
    lax.fori_loop(tiles // 2, tiles, piece, 0)
    gram_ref[:RANK] = reduce_end("slab", slabs, sums_two, basis_two)
    by_part = matched(products[:snap_rows], 3 * SNAPS)
    lines = [
        by_part[3 * s : 3 * s + 1] + by_part[3 * s + 1 : 3 * s + 2] + by_part[3 * s + 2 : 3 * s + 3]
        for s in range(SNAPS)
    ]

    row = iota((SUB, LANES), 0)
    lane = iota((SUB, LANES), 1)
    result = jnp.zeros((SUB, LANES), F32)
    for s in range(SNAPS):
        result = jnp.where(row == s, lines[s], result)
    for a in range(SNAPS):
        for b in range(a + 1):
            result = jnp.where((row == a) & (lane == RANK + b), jnp.sum(squares[3 * a + b]), result)
    late_sums_one[0] = result
    late = reduce_start("tile", tiles, late_sums_one, one_send.at[1], one_recv.at[1])
    for copy in late:
        copy.start()
    late_sums_two[0] = reduce_end("tile", tiles, late_sums_one, late)
    late = reduce_start("slab", slabs, late_sums_two, two_send.at[1], two_recv.at[1])
    for copy in late:
        copy.start()
    gram_ref[RANK:] = reduce_end("slab", slabs, late_sums_two, late)

    for k in range(SNAPS):
        for d in range(1, tiles):
            bulk(k, d).wait_send()


def mix(row_scale, low, sigma_ref, rotation_ref, factor_ref, weight_ref, snap_ref):
    rows = GRAM_ROWS
    row = iota((rows, LANES), 0)
    lane = iota((rows, LANES), 1)
    weight = jnp.where(iota((1, LANES), 1) < RANK, sigma_ref[...], 1.0)
    wide_weight = jnp.broadcast_to(weight, (LANES, LANES))
    low = low * weight * wide_weight.T[:rows]
    high = jnp.concatenate([low, jnp.zeros((LANES - rows, LANES), F32)], axis=0).T[:rows]
    gram = jnp.where((row < RANK) & (lane >= RANK), high, low)
    upper_right = (row >= RANK) & (lane > row)
    gram = jnp.where(upper_right, high, gram)
    gram = jnp.where((lane < K) & (row < K), gram, 0.0)
    start = gram + jnp.where((lane == row + 64) | ((lane == row) & (row >= K)), 1.0, 0.0)
    blocks = [start[SUB * b : SUB * b + SUB] for b in range(rows // SUB)]
    sub = iota((SUB, LANES), 0)
    for i in range(K):
        at, inner = divmod(i, SUB)
        pivot_row = blocks[at][inner : inner + 1, :]
        scaled = pivot_row / pivot_row[:, i : i + 1]
        for b in range(at, rows // SUB):
            column = blocks[b][:, i : i + 1]
            update = column * scaled
            if b == at:
                update = jnp.where(sub > inner, update, 0.0)
            blocks[b] = blocks[b] - update
    done = jnp.concatenate(blocks, axis=0)
    pivots = jnp.sum(jnp.where(lane == row, done, 0.0), axis=1, keepdims=True)
    done = done / jnp.sqrt(pivots)
    factor = jnp.where(lane >= row, done, 0.0) * (1.0 / row_scale)
    factor_ref[...] = factor[:K, :K]
    inverse = jnp.where(row < K, done, 0.0)
    mixed = row_scale * lax.dot_general(
        rotation_ref[...],
        inverse,
        (((0,), (0,)), ((), ())),
        precision=HIGHEST,
        preferred_element_type=F32,
    )
    mixed = mixed[:RANK]
    sigma_lane = jnp.concatenate([jnp.zeros((1, 64), F32), sigma_ref[:, :64]], axis=1)
    spread = ((iota((LANES, WIDE), 0) - 64) == iota((LANES, WIDE), 1) // SUB).astype(BF16)
    same = iota((WIDE, WIDE), 0) % SUB == iota((WIDE, WIDE), 1) % SUB
    for part, values in enumerate(pieces(mixed * sigma_lane, 2)):
        wide = jnp.dot(values, spread, preferred_element_type=F32)
        tall = jnp.broadcast_to(wide[:, None, :], (RANK, SUB, WIDE)).reshape(WIDE, WIDE)
        weight_ref[WIDE * part : WIDE * part + WIDE] = jnp.where(same, tall, 0.0).astype(BF16)
    for s in range(SNAPS):
        column = mixed[:, 64 + RANK + s : 64 + RANK + s + 1]
        snap_ref[s] = jnp.broadcast_to(column[:, :, None], (RANK, SUB, LANES))


def rotate_kernel(
    row_scale,
    gram_ref,
    sigma_ref,
    rotation_ref,
    modes_hbm,
    snaps,
    flow,
    advanced,
    factor_ref,
    new_modes,
    modes,
    weight_ref,
    snap_ref,
    staged,
    flow_sem,
    out_sem,
    mode_sem,
):
    planes, tiles = modes.shape[1], modes.shape[2]

    def mode_copy(plane):
        return pltpu.make_async_copy(modes_hbm.at[:, plane], modes.at[:, plane], mode_sem.at[plane])

    for plane in range(planes):
        mode_copy(plane).start()
    passing = pltpu.make_async_copy(flow, advanced, flow_sem)
    passing.start()
    mix(row_scale, gram_ref[...], sigma_ref, rotation_ref, factor_ref, weight_ref, snap_ref)
    width = snaps.shape[2]

    def out_copy(plane, slot):
        return pltpu.make_async_copy(staged.at[slot], new_modes.at[:, plane], out_sem.at[slot])

    def plane_step(plane, carry):
        slot = lax.rem(plane, 2)

        @pl.when(plane >= 2)
        def _():
            out_copy(plane - 2, slot).wait()

        mode_copy(plane).wait()
        c, w = lax.div(plane, width), lax.rem(plane, width)
        for t in range(0, tiles, 2):
            both = jnp.dot(weight_ref[...], wide_pair(modes, plane, t), preferred_element_type=F32)
            both = both[:WIDE] + both[WIDE:]
            for half in range(2):
                value = both[:, LANES * half : LANES * half + LANES].reshape(RANK, SUB, LANES)
                for s in range(SNAPS):
                    value = value + snap_ref[s] * snaps[s, c, w, t + half][None]
                staged[slot, :, t + half] = value.astype(BF16)
        out_copy(plane, slot).start()
        return carry

    lax.fori_loop(0, planes, plane_step, 0)
    for plane in (planes - 2, planes - 1):
        out_copy(plane, plane % 2).wait()
    passing.wait()


def hbm_spec():
    return pl.BlockSpec(memory_space=pltpu.HBM)


def vmem_spec():
    return pl.BlockSpec(memory_space=pltpu.VMEM)


def shards(slabs, tiles, velocity, viscosity, basis, sigma, rotation):
    _, parts, width, deep, lanes = basis.shape
    planes, deep_tiles = parts * width, deep // SUB
    count = velocity.shape[1]
    row_scale = math.sqrt(planes * deep * lanes * slabs * tiles)
    modes_hbm = basis.reshape(RANK, planes, deep_tiles, SUB, LANES)
    flow_shape = (3, count, 2, SUB, LANES)
    flow, gram, snaps = pl.pallas_call(
        functools.partial(exchange_kernel, slabs, tiles),
        in_specs=[hbm_spec(), hbm_spec(), hbm_spec()],
        out_specs=[vmem_spec(), vmem_spec(), vmem_spec()],
        out_shape=[
            pltpu.VMEM(flow_shape, F32),
            pltpu.VMEM((GRAM_ROWS, LANES), F32),
            pltpu.VMEM((SNAPS, parts, width, deep_tiles, SUB, LANES), F32),
        ],
        scratch_shapes=[
            pltpu.VMEM(modes_hbm.shape, BF16),
            pltpu.VMEM((2, 3, count + 2, 2, SUB, LANES), F32),
            pltpu.VMEM((count, 2, SUB, LANES), F32),
            pltpu.VMEM((2, 3, count, LANES), F32),
            pltpu.VMEM((2, 3, count, LANES), F32),
            pltpu.VMEM((2, 3, count, LANES), F32),
            pltpu.VMEM((2, 3, count, LANES), F32),
            pltpu.VMEM((WIDE, WIDE), F32),
            pltpu.VMEM((9, SUB, LANES), F32),
            pltpu.VMEM((1 + tiles, RANK, LANES), F32),
            pltpu.VMEM((1 + slabs, RANK, LANES), F32),
            pltpu.VMEM((1 + tiles, SUB, LANES), F32),
            pltpu.VMEM((1 + slabs, SUB, LANES), F32),
            pltpu.SemaphoreType.DMA((2,)),
            pltpu.SemaphoreType.DMA((planes,)),
            pltpu.SemaphoreType.DMA((SNAPS,)),
            pltpu.SemaphoreType.DMA((2, 4)),
            pltpu.SemaphoreType.DMA((2, 4)),
            pltpu.SemaphoreType.DMA((SNAPS, tiles)),
            pltpu.SemaphoreType.DMA((SNAPS, tiles)),
            pltpu.SemaphoreType.DMA((2, tiles)),
            pltpu.SemaphoreType.DMA((2, tiles)),
            pltpu.SemaphoreType.DMA((2, slabs)),
            pltpu.SemaphoreType.DMA((2, slabs)),
        ],
        compiler_params=pltpu.CompilerParams(
            collective_id=0, has_side_effects=True, vmem_limit_bytes=EXCHANGE_VMEM
        ),
        name="exchange",
    )(velocity.reshape(flow_shape), viscosity.reshape(count, 2, SUB, LANES), modes_hbm)
    sigma_row = jnp.pad(sigma[None], ((0, 0), (0, LANES - RANK)))
    rotation_wide = jnp.pad(rotation, ((0, GRAM_ROWS - K), (0, LANES - RANK)))
    advanced, factor, rotated = pl.pallas_call(
        functools.partial(rotate_kernel, row_scale),
        in_specs=[vmem_spec(), vmem_spec(), vmem_spec(), hbm_spec(), vmem_spec(), vmem_spec()],
        out_specs=[hbm_spec(), vmem_spec(), hbm_spec()],
        out_shape=[
            jax.ShapeDtypeStruct(flow_shape, F32),
            jax.ShapeDtypeStruct((K, K), F32),
            jax.ShapeDtypeStruct(modes_hbm.shape, BF16),
        ],
        scratch_shapes=[
            pltpu.VMEM(modes_hbm.shape, BF16),
            pltpu.VMEM((2 * WIDE, WIDE), BF16),
            pltpu.VMEM((SNAPS, RANK, SUB, LANES), F32),
            pltpu.VMEM((2, RANK, deep_tiles, SUB, LANES), BF16),
            pltpu.SemaphoreType.DMA,
            pltpu.SemaphoreType.DMA((2,)),
            pltpu.SemaphoreType.DMA((planes,)),
        ],
        compiler_params=pltpu.CompilerParams(vmem_limit_bytes=ROTATE_VMEM),
        name="rotate",
    )(gram, sigma_row, rotation_wide, modes_hbm, snaps, flow)
    return (advanced.reshape(velocity.shape), factor, rotated.reshape(basis.shape))


def solution(mesh):
    in_specs = (
        P(None, "slab", "tile", None),
        P("slab", "tile", None),
        P(None, None, ("slab", "tile"), None, None),
        P(),
        P(),
    )
    out_specs = (P(None, "slab", "tile", None), P(), P(None, None, ("slab", "tile"), None, None))
    return jax.shard_map(
        functools.partial(shards, mesh.shape["slab"], mesh.shape["tile"]),
        mesh=mesh,
        in_specs=in_specs,
        out_specs=out_specs,
        check_vma=False,
    )
```

```python
import functools
import math

import jax
import jax.numpy as jnp
from jax import lax
from jax.experimental import pallas as pl
from jax.experimental.pallas import tpu as pltpu
from jax.sharding import PartitionSpec as P

step_size = 0.25
RANK = 32
SNAPS = 3
K = RANK + SNAPS
SUB = 8
LANES = 128
WIDE = RANK * SUB
F32 = jnp.float32
BF16 = jnp.bfloat16
HIGHEST = lax.Precision.HIGHEST
MESH = pl.DeviceIdType.MESH
GRAM_ROWS = 40
EXCHANGE_VMEM = 63_700_000
ROTATE_VMEM = 50 << 20


def iota(shape, dim):
    return lax.broadcasted_iota(jnp.int32, shape, dim)


def pieces(values, count):
    parts = []
    for _ in range(count):
        part = values.astype(BF16)
        parts.append(part)
        values = values - part.astype(F32)
    return parts


def matched(product, rows):
    same = iota(product.shape, 0) % SUB == iota(product.shape, 1) % SUB
    summed = jnp.where(same, product, 0.0).reshape(rows, SUB, WIDE).sum(1)
    pick = (iota((WIDE, LANES), 0) // SUB == iota((WIDE, LANES), 1)).astype(F32)
    return jnp.dot(summed, pick, precision=HIGHEST, preferred_element_type=F32)


def wide_pair(ref, *index):
    *front, tile = index
    left = ref[(slice(None), *front, tile)].reshape(WIDE, LANES)
    right = ref[(slice(None), *front, tile + 1)].reshape(WIDE, LANES)
    return jnp.concatenate([left, right], axis=1)


def advance_planes(padded, low, high, viscosity, store):
    count = viscosity.shape[0]
    depth = 2 * SUB
    row = iota((depth, LANES), 0)
    lane = iota((depth, LANES), 1)

    def plane(x, carry):
        def at(c, p):
            return padded[c, p].reshape(depth, LANES)

        flow = [at(c, x + 1) for c in range(3)]
        nu = viscosity[x].reshape(depth, LANES)
        for c in range(3):
            centre = flow[c]
            forward_x, backward_x = at(c, x + 2), at(c, x)
            forward_z = jnp.where(row == depth - 1, high[c, pl.ds(x, 1)], pltpu.roll(centre, depth - 1, 0))
            backward_z = jnp.where(row == 0, low[c, pl.ds(x, 1)], pltpu.roll(centre, 1, 0))
            above_y = jnp.where(lane == LANES - 1, 0.0, pltpu.roll(centre, LANES - 1, 1))
            below_y = jnp.where(lane == 0, 0.0, pltpu.roll(centre, 1, 1))
            laplace = forward_x + backward_x + forward_z + backward_z + above_y + below_y - 6.0 * centre
            carried = (
                flow[0] * (forward_x - backward_x)
                + flow[1] * (above_y - below_y)
                + flow[2] * (forward_z - backward_z)
            )
            store(c, x, centre + step_size * (nu * laplace - 0.5 * carried))
        return carry

    lax.fori_loop(0, count, plane, 0)


def exchange_kernel(
    slabs,
    tiles,
    vel_hbm,
    nu_hbm,
    modes_hbm,
    sigma_ref,
    advanced,
    early_ref,
    late_ref,
    snaps,
    modes,
    flow,
    nu,
    low,
    high,
    low_edge,
    high_edge,
    products,
    squares,
    sums_one,
    sums_two,
    late_sums_one,
    late_sums_two,
    weight_row,
    load_sem,
    mode_sem,
    own_sem,
    face_send,
    face_recv,
    bulk_send,
    bulk_recv,
    one_send,
    one_recv,
    two_send,
    two_recv,
):
    slab, tile = lax.axis_index("slab"), lax.axis_index("tile")
    planes = modes.shape[1]
    width = snaps.shape[2]
    count = nu.shape[0]

    def shifted(index, by, size):
        return lax.rem(index + by + size, size)

    loads = [
        pltpu.make_async_copy(vel_hbm, flow.at[0, :, 1 : count + 1], load_sem.at[0]),
        pltpu.make_async_copy(nu_hbm, nu, load_sem.at[1]),
    ]
    for copy in loads:
        copy.start()

    barrier = pltpu.get_barrier_semaphore()
    for d in range(1, tiles):
        pl.semaphore_signal(barrier, inc=1, device_id={"tile": shifted(tile, d, tiles)}, device_id_type=MESH)
    for d in range(1, slabs):
        pl.semaphore_signal(barrier, inc=1, device_id={"slab": shifted(slab, d, slabs)}, device_id_type=MESH)

    def mode_copy(plane):
        return pltpu.make_async_copy(modes_hbm.at[:, plane], modes.at[:, plane], mode_sem.at[plane])

    for copy in loads:
        copy.wait()
    for plane in range(planes):
        mode_copy(plane).start()

    def edges(x, carry):
        for c in range(3):
            low_edge[0, c, pl.ds(x, 1)] = flow[0, c, x + 1, 0, 0:1]
            high_edge[0, c, pl.ds(x, 1)] = flow[0, c, x + 1, 1, SUB - 1 : SUB]
        return carry

    lax.fori_loop(0, count, edges, 0)
    pl.semaphore_wait(barrier, tiles + slabs - 2)

    def faces(step):
        up_x, down_x = {"slab": shifted(slab, 1, slabs)}, {"slab": shifted(slab, -1, slabs)}
        up_z, down_z = {"tile": shifted(tile, 1, tiles)}, {"tile": shifted(tile, -1, tiles)}
        moves = [
            (low_edge.at[step], high.at[step], down_z),
            (high_edge.at[step], low.at[step], up_z),
            (flow.at[step, :, count], flow.at[step, :, 0], up_x),
            (flow.at[step, :, 1], flow.at[step, :, count + 1], down_x),
        ]
        return [
            pltpu.make_async_remote_copy(
                src_ref=source,
                dst_ref=target,
                send_sem=face_send.at[step, i],
                recv_sem=face_recv.at[step, i],
                device_id=device,
                device_id_type=MESH,
            )
            for i, (source, target, device) in enumerate(moves)
        ]

    def strip(k, owner):
        start = owner * width
        if k == 2:
            return advanced.at[:, pl.ds(start, width)]
        return flow.at[k, :, pl.ds(start + 1, width)]

    def bulk(k, d):
        owner = shifted(tile, d, tiles)
        return pltpu.make_async_remote_copy(
            src_ref=strip(k, owner),
            dst_ref=snaps.at[k, :, :, pl.ds(2 * tile, 2)],
            send_sem=bulk_send.at[k, d],
            recv_sem=bulk_recv.at[k, d],
            device_id={"tile": owner},
            device_id_type=MESH,
        )

    def own(k):
        return pltpu.make_async_copy(strip(k, tile), snaps.at[k, :, :, pl.ds(2 * tile, 2)], own_sem.at[k])

    def send_strips(k):
        for d in range(1, tiles):
            bulk(k, d).start()
        own(k).start()

    def gram_planes(first, last):
        def plane_step(plane, carry):
            mode_copy(plane).wait()
            columns = jnp.concatenate(
                [wide_pair(modes, plane, t) for t in range(0, modes.shape[2], 2)], axis=1
            )
            products[...] += lax.dot_general(
                columns, columns, (((1,), (1,)), ((), ())), preferred_element_type=F32
            )
            return carry

        lax.fori_loop(first, last, plane_step, 0)

    def reduce_start(axis, size, sums, send, recv):
        me = lax.axis_index(axis)
        return [
            pltpu.make_async_remote_copy(
                src_ref=sums.at[0],
                dst_ref=sums.at[1 + me],
                send_sem=send.at[d],
                recv_sem=recv.at[d],
                device_id={axis: shifted(me, d, size)},
                device_id_type=MESH,
            )
            for d in range(1, size)
        ]

    def reduce_end(axis, size, sums, copies):
        me = lax.axis_index(axis)
        sums[1 + me] = sums[0]
        for copy in copies:
            copy.wait()
        total = sums[1]
        for i in range(1, size):
            total = total + sums[1 + i]
        return total

    first_faces = faces(0)
    for copy in first_faces:
        copy.start()
    send_strips(0)
    weight_row[...] = jnp.zeros_like(weight_row)
    weight_row[:, :RANK] = sigma_ref[...]
    products[...] = jnp.zeros_like(products)
    squares[...] = jnp.zeros_like(squares)
    gram_planes(0, planes)
    sums_one[0] = matched(products[...], RANK)
    basis_one = reduce_start("tile", tiles, sums_one, one_send.at[0], one_recv.at[0])
    for copy in basis_one:
        copy.start()
    for copy in first_faces:
        copy.wait()

    def store_first(c, x, value):
        flow[1, c, x + 1] = value.reshape(2, SUB, LANES)
        low_edge[1, c, pl.ds(x, 1)] = value[0:1]
        high_edge[1, c, pl.ds(x, 1)] = value[2 * SUB - 1 :]

    advance_planes(flow.at[0], low.at[0], high.at[0], nu, store_first)
    second_faces = faces(1)
    for copy in second_faces:
        copy.start()
    send_strips(1)
    sums_two[0] = reduce_end("tile", tiles, sums_one, basis_one)
    basis_two = reduce_start("slab", slabs, sums_two, two_send.at[0], two_recv.at[0])
    for copy in basis_two:
        copy.start()
    for copy in second_faces:
        copy.wait()

    def store_second(c, x, value):
        advanced[c, x] = value.reshape(2, SUB, LANES)

    advance_planes(flow.at[1], low.at[1], high.at[1], nu, store_second)
    send_strips(2)

    weight = weight_row[...]
    early_row = iota((RANK, LANES), 0)
    early_lane = iota((RANK, LANES), 1)
    tall_weight = jnp.broadcast_to(weight, (LANES, LANES)).T[:RANK]
    early_ref[...] = reduce_end("slab", slabs, sums_two, basis_two) * weight * tall_weight + (
        early_lane == early_row + 64
    ).astype(F32)

    def eliminate(i, carry):
        block = early_ref[...]
        pivot_row = early_ref[pl.ds(i, 1)]
        column = jnp.sum(jnp.where(early_lane == i, block, 0.0), axis=1, keepdims=True)
        pivot = jnp.sum(jnp.where(early_lane[:1] == i, pivot_row, 0.0), axis=1, keepdims=True)
        update = column * (pivot_row / pivot)
        early_ref[...] = block - jnp.where(early_row > i, update, 0.0)
        return carry

    lax.fori_loop(0, RANK, eliminate, 0)
    eliminated = early_ref[...]
    pivots = jnp.sum(jnp.where(early_lane == early_row, eliminated, 0.0), axis=1, keepdims=True)
    eliminated = eliminated / jnp.sqrt(pivots)
    early_ref[...] = jnp.where((early_lane >= early_row) | (early_lane >= 64), eliminated, 0.0)

    snap_rows = 3 * SNAPS * SUB
    products[:snap_rows] = jnp.zeros((snap_rows, WIDE), F32)

    def gram_pieces(group):
        def piece(turn, carry):
            @pl.when(turn == 0)
            def _():
                for k in group:
                    own(k).wait()

            @pl.when(turn > 0)
            def _():
                for k in group:
                    bulk(k, turn).wait_recv()

            at = 2 * shifted(tile, -turn, tiles)
            columns = jnp.concatenate([wide_pair(modes, p, at) for p in range(planes)], axis=1)
            rows = []
            for k in group:
                flat = jnp.concatenate(
                    [
                        snaps[k, p // width, p % width, at + h]
                        for p in range(planes)
                        for h in range(2)
                    ],
                    axis=1,
                )
                rows.extend(pieces(flat, 3))
            first, last = 3 * SUB * group[0], 3 * SUB * (group[-1] + 1)
            products[first:last] += lax.dot_general(
                jnp.concatenate(rows, axis=0),
                columns,
                (((1,), (1,)), ((), ())),
                preferred_element_type=F32,
            )
            for a in group:
                for b in range(a + 1):
                    total = jnp.zeros((SUB, LANES), F32)
                    for p in range(planes):
                        for h in range(2):
                            c, w = divmod(p, width)
                            total = total + snaps[a, c, w, at + h] * snaps[b, c, w, at + h]
                    squares[3 * a + b] += total
            return carry

        lax.fori_loop(0, tiles, piece, 0)

    gram_pieces((0, 1))
    gram_pieces((2,))
    by_part = matched(products[:snap_rows], 3 * SNAPS)
    row = iota((SUB, LANES), 0)
    lane = iota((SUB, LANES), 1)
    result = jnp.zeros((SUB, LANES), F32)
    for s in range(SNAPS):
        line = by_part[3 * s : 3 * s + 1] + by_part[3 * s + 1 : 3 * s + 2] + by_part[3 * s + 2 : 3 * s + 3]
        result = jnp.where(row == s, line, result)
    for a in range(SNAPS):
        for b in range(a + 1):
            here = ((row == a) & (lane == RANK + b)) | ((row == b) & (lane == RANK + a))
            result = jnp.where(here, jnp.sum(squares[3 * a + b]), result)
    late_sums_one[0] = result
    late = reduce_start("tile", tiles, late_sums_one, one_send.at[1], one_recv.at[1])
    for copy in late:
        copy.start()
    late_sums_two[0] = reduce_end("tile", tiles, late_sums_one, late)
    late = reduce_start("slab", slabs, late_sums_two, two_send.at[1], two_recv.at[1])
    for copy in late:
        copy.start()
    late_ref[...] = reduce_end("slab", slabs, late_sums_two, late)

    for k in range(SNAPS):
        for d in range(1, tiles):
            bulk(k, d).wait_send()


def mix(row_scale, early_ref, late_ref, sigma_row, rotation_ref, factor_ref, weight_ref, snap_ref):
    row = iota((GRAM_ROWS, LANES), 0)
    lane = iota((GRAM_ROWS, LANES), 1)
    sub = iota((SUB, LANES), 0)
    short = iota((SUB, LANES), 1)
    top = early_ref[...]
    inverse_top = jnp.where(lane[:RANK] >= 64, top, 0.0)
    late = late_ref[...] * jnp.where(short < RANK, sigma_row, 1.0)
    cross = pltpu.roll(jnp.where(short < RANK, late, 0.0), 64, 1)
    placed = jnp.concatenate(
        [jnp.zeros((RANK, LANES), F32), cross, jnp.zeros((LANES - GRAM_ROWS, LANES), F32)], axis=0
    )
    lanes_both = (((1,), (1,)), ((), ()))
    top = top + lax.dot_general(
        inverse_top, placed, lanes_both, precision=HIGHEST, preferred_element_type=F32
    )
    weights = lax.dot_general(
        cross, inverse_top, lanes_both, precision=HIGHEST, preferred_element_type=F32
    )
    bottom = jnp.where(sub < SNAPS, late, 0.0) + (
        (short == sub + 64 + RANK) | ((short == sub + RANK) & (sub >= SNAPS))
    ).astype(F32)
    bottom = bottom - jnp.dot(weights, top, precision=HIGHEST, preferred_element_type=F32)
    for i in range(SNAPS):
        pivot_row = bottom[i : i + 1]
        scaled = pivot_row / pivot_row[:, RANK + i : RANK + i + 1]
        update = bottom[:, RANK + i : RANK + i + 1] * scaled
        bottom = bottom - jnp.where(sub > i, update, 0.0)
    pivots = jnp.sum(jnp.where(short == sub + RANK, bottom, 0.0), axis=1, keepdims=True)
    done = jnp.concatenate([top, bottom / jnp.sqrt(pivots)], axis=0)
    factor = jnp.where(lane >= row, done, 0.0) * (1.0 / row_scale)
    factor_ref[...] = factor[:K, :K]
    inverse = jnp.where(row < K, done, 0.0)
    mixed = row_scale * jnp.dot(
        rotation_ref[:, :GRAM_ROWS], inverse, precision=HIGHEST, preferred_element_type=F32
    )
    sigma_lane = pltpu.roll(sigma_row, 64, 1)
    spread = ((iota((LANES, WIDE), 0) - 64) == iota((LANES, WIDE), 1) // SUB).astype(BF16)
    same = iota((WIDE, WIDE), 0) % SUB == iota((WIDE, WIDE), 1) % SUB
    for part, values in enumerate(pieces(mixed * sigma_lane, 2)):
        wide = jnp.dot(values, spread, preferred_element_type=F32)
        tall = jnp.broadcast_to(wide[:, None, :], (RANK, SUB, WIDE)).reshape(WIDE, WIDE)
        weight_ref[WIDE * part : WIDE * part + WIDE] = jnp.where(same, tall, 0.0).astype(BF16)
    for s in range(SNAPS):
        column = mixed[:, 64 + RANK + s : 64 + RANK + s + 1]
        snap_ref[s] = jnp.broadcast_to(column[:, :, None], (RANK, SUB, LANES))


def rotate_kernel(
    row_scale,
    early_ref,
    late_ref,
    sigma_ref,
    rotation_ref,
    modes_hbm,
    snaps,
    flow,
    advanced,
    factor_ref,
    new_modes,
    modes,
    sigma_row,
    rotation_wide,
    weight_ref,
    snap_ref,
    staged,
    flow_sem,
    out_sem,
    mode_sem,
):
    planes, tiles = modes.shape[1], modes.shape[2]

    def mode_copy(plane):
        return pltpu.make_async_copy(modes_hbm.at[:, plane], modes.at[:, plane], mode_sem.at[plane])

    for plane in range(planes):
        mode_copy(plane).start()
    passing = pltpu.make_async_copy(flow, advanced, flow_sem)
    passing.start()
    sigma_row[...] = jnp.zeros_like(sigma_row)
    sigma_row[:, :RANK] = sigma_ref[...]
    rotation_wide[...] = jnp.zeros_like(rotation_wide)
    rotation_wide[:, :K] = rotation_ref[...]
    mix(
        row_scale, early_ref, late_ref, sigma_row[...], rotation_wide, factor_ref, weight_ref, snap_ref
    )
    width = snaps.shape[2]

    def out_copy(plane, slot):
        return pltpu.make_async_copy(staged.at[slot], new_modes.at[:, plane], out_sem.at[slot])

    def plane_step(plane, carry):
        slot = lax.rem(plane, 2)

        @pl.when(plane >= 2)
        def _():
            out_copy(plane - 2, slot).wait()

        mode_copy(plane).wait()
        c, w = lax.div(plane, width), lax.rem(plane, width)
        for t in range(0, tiles, 2):
            both = jnp.dot(weight_ref[...], wide_pair(modes, plane, t), preferred_element_type=F32)
            both = both[:WIDE] + both[WIDE:]
            for half in range(2):
                value = both[:, LANES * half : LANES * half + LANES].reshape(RANK, SUB, LANES)
                for s in range(SNAPS):
                    value = value + snap_ref[s] * snaps[s, c, w, t + half][None]
                staged[slot, :, t + half] = value.astype(BF16)
        out_copy(plane, slot).start()
        return carry

    lax.fori_loop(0, planes, plane_step, 0)
    for plane in (planes - 2, planes - 1):
        out_copy(plane, plane % 2).wait()
    passing.wait()


def hbm_spec():
    return pl.BlockSpec(memory_space=pltpu.HBM)


def vmem_spec():
    return pl.BlockSpec(memory_space=pltpu.VMEM)


def shards(slabs, tiles, velocity, viscosity, basis, sigma, rotation):
    _, parts, width, deep, lanes = basis.shape
    planes, deep_tiles = parts * width, deep // SUB
    count = velocity.shape[1]
    row_scale = math.sqrt(planes * deep * lanes * slabs * tiles)
    modes_hbm = basis.reshape(RANK, planes, deep_tiles, SUB, LANES)
    flow_shape = (3, count, 2, SUB, LANES)
    sigma_row = sigma.reshape(1, RANK)
    flow, early, late, snaps = pl.pallas_call(
        functools.partial(exchange_kernel, slabs, tiles),
        in_specs=[hbm_spec(), hbm_spec(), hbm_spec(), vmem_spec()],
        out_specs=[vmem_spec()] * 4,
        out_shape=[
            pltpu.VMEM(flow_shape, F32),
            pltpu.VMEM((RANK, LANES), F32),
            pltpu.VMEM((SUB, LANES), F32),
            pltpu.VMEM((SNAPS, parts, width, deep_tiles, SUB, LANES), F32),
        ],
        scratch_shapes=[
            pltpu.VMEM(modes_hbm.shape, BF16),
            pltpu.VMEM((2, 3, count + 2, 2, SUB, LANES), F32),
            pltpu.VMEM((count, 2, SUB, LANES), F32),
            pltpu.VMEM((2, 3, count, LANES), F32),
            pltpu.VMEM((2, 3, count, LANES), F32),
            pltpu.VMEM((2, 3, count, LANES), F32),
            pltpu.VMEM((2, 3, count, LANES), F32),
            pltpu.VMEM((WIDE, WIDE), F32),
            pltpu.VMEM((9, SUB, LANES), F32),
            pltpu.VMEM((1 + tiles, RANK, LANES), F32),
            pltpu.VMEM((1 + slabs, RANK, LANES), F32),
            pltpu.VMEM((1 + tiles, SUB, LANES), F32),
            pltpu.VMEM((1 + slabs, SUB, LANES), F32),
            pltpu.VMEM((1, LANES), F32),
            pltpu.SemaphoreType.DMA((2,)),
            pltpu.SemaphoreType.DMA((planes,)),
            pltpu.SemaphoreType.DMA((SNAPS,)),
            pltpu.SemaphoreType.DMA((2, 4)),
            pltpu.SemaphoreType.DMA((2, 4)),
            pltpu.SemaphoreType.DMA((SNAPS, tiles)),
            pltpu.SemaphoreType.DMA((SNAPS, tiles)),
            pltpu.SemaphoreType.DMA((2, tiles)),
            pltpu.SemaphoreType.DMA((2, tiles)),
            pltpu.SemaphoreType.DMA((2, slabs)),
            pltpu.SemaphoreType.DMA((2, slabs)),
        ],
        compiler_params=pltpu.CompilerParams(
            collective_id=0, has_side_effects=True, vmem_limit_bytes=EXCHANGE_VMEM
        ),
        name="exchange",
    )(velocity.reshape(flow_shape), viscosity.reshape(count, 2, SUB, LANES), modes_hbm, sigma_row)
    advanced, factor, rotated = pl.pallas_call(
        functools.partial(rotate_kernel, row_scale),
        in_specs=[vmem_spec()] * 4 + [hbm_spec(), vmem_spec(), vmem_spec()],
        out_specs=[hbm_spec(), vmem_spec(), hbm_spec()],
        out_shape=[
            jax.ShapeDtypeStruct(flow_shape, F32),
            jax.ShapeDtypeStruct((K, K), F32),
            jax.ShapeDtypeStruct(modes_hbm.shape, BF16),
        ],
        scratch_shapes=[
            pltpu.VMEM(modes_hbm.shape, BF16),
            pltpu.VMEM((1, LANES), F32),
            pltpu.VMEM((RANK, LANES), F32),
            pltpu.VMEM((2 * WIDE, WIDE), BF16),
            pltpu.VMEM((SNAPS, RANK, SUB, LANES), F32),
            pltpu.VMEM((2, RANK, deep_tiles, SUB, LANES), BF16),
            pltpu.SemaphoreType.DMA,
            pltpu.SemaphoreType.DMA((2,)),
            pltpu.SemaphoreType.DMA((planes,)),
        ],
        compiler_params=pltpu.CompilerParams(vmem_limit_bytes=ROTATE_VMEM),
        name="rotate",
    )(early, late, sigma_row, rotation.T, modes_hbm, snaps, flow)
    return (advanced.reshape(velocity.shape), factor, rotated.reshape(basis.shape))


def solution(mesh):
    in_specs = (
        P(None, "slab", "tile", None),
        P("slab", "tile", None),
        P(None, None, ("slab", "tile"), None, None),
        P(),
        P(),
    )
    out_specs = (P(None, "slab", "tile", None), P(), P(None, None, ("slab", "tile"), None, None))
    return jax.shard_map(
        functools.partial(shards, mesh.shape["slab"], mesh.shape["tile"]),
        mesh=mesh,
        in_specs=in_specs,
        out_specs=out_specs,
        check_vma=False,
    )
```

```python
import functools
import math

import jax
import jax.numpy as jnp
from jax import lax
from jax.experimental import pallas as pl
from jax.experimental.pallas import tpu as pltpu
from jax.sharding import PartitionSpec as P

step_size = 0.25
RANK = 32
SNAPS = 3
K = RANK + SNAPS
SUB = 8
LANES = 128
WIDE = RANK * SUB
F32 = jnp.float32
BF16 = jnp.bfloat16
HIGHEST = lax.Precision.HIGHEST
MESH = pl.DeviceIdType.MESH
GRAM_ROWS = 40
CORES = 2
HALVES = 2
EXCHANGE_VMEM = 63_700_000
ROTATE_VMEM = 50 << 20


def iota(shape, dim):
    return lax.broadcasted_iota(jnp.int32, shape, dim)


def pieces(values, count):
    parts = []
    for _ in range(count):
        part = values.astype(BF16)
        parts.append(part)
        values = values - part.astype(F32)
    return parts


def matched(product, rows):
    same = iota(product.shape, 0) % SUB == iota(product.shape, 1) % SUB
    summed = jnp.where(same, product, 0.0).reshape(rows, SUB, WIDE).sum(1)
    pick = (iota((WIDE, LANES), 0) // SUB == iota((WIDE, LANES), 1)).astype(F32)
    return jnp.dot(summed, pick, precision=HIGHEST, preferred_element_type=F32)


def wide_pair(ref, *index):
    *front, tile = index
    left = ref[(slice(None), *front, tile)].reshape(WIDE, LANES)
    right = ref[(slice(None), *front, tile + 1)].reshape(WIDE, LANES)
    return jnp.concatenate([left, right], axis=1)


def advance_planes(padded, low, high, viscosity, store):
    count = viscosity.shape[0]
    depth = 2 * SUB
    row = iota((depth, LANES), 0)
    lane = iota((depth, LANES), 1)

    def plane(x, carry):
        def at(c, p):
            return padded[c, p].reshape(depth, LANES)

        flow = [at(c, x + 1) for c in range(3)]
        nu = viscosity[x].reshape(depth, LANES)
        for c in range(3):
            centre = flow[c]
            forward_x, backward_x = at(c, x + 2), at(c, x)
            forward_z = jnp.where(row == depth - 1, high[c, pl.ds(x, 1)], pltpu.roll(centre, depth - 1, 0))
            backward_z = jnp.where(row == 0, low[c, pl.ds(x, 1)], pltpu.roll(centre, 1, 0))
            above_y = jnp.where(lane == LANES - 1, 0.0, pltpu.roll(centre, LANES - 1, 1))
            below_y = jnp.where(lane == 0, 0.0, pltpu.roll(centre, 1, 1))
            laplace = forward_x + backward_x + forward_z + backward_z + above_y + below_y - 6.0 * centre
            carried = (
                flow[0] * (forward_x - backward_x)
                + flow[1] * (above_y - below_y)
                + flow[2] * (forward_z - backward_z)
            )
            store(c, x, centre + step_size * (nu * laplace - 0.5 * carried))
        return carry

    lax.fori_loop(0, count, plane, 0)


def exchange_kernel(
    slabs,
    tiles,
    vel_hbm,
    nu_hbm,
    modes_hbm,
    sigma_ref,
    advanced,
    early_ref,
    late_ref,
    snaps,
    modes,
    flow,
    nu,
    low,
    high,
    low_edge,
    high_edge,
    products,
    squares,
    sums_one,
    sums_two,
    late_sums_one,
    late_sums_two,
    weight_row,
    load_sem,
    mode_sem,
    own_sem,
    face_send,
    face_recv,
    bulk_send,
    bulk_recv,
    one_send,
    one_recv,
    two_send,
    two_recv,
):
    slab, tile = lax.axis_index("slab"), lax.axis_index("tile")
    planes = modes.shape[1]
    width = snaps.shape[2]
    count = nu.shape[0]

    def shifted(index, by, size):
        return lax.rem(index + by + size, size)

    block = HALVES * CORES
    near, far = slabs // HALVES, HALVES * tiles
    line, half, core = lax.div(slab, block), lax.rem(lax.div(slab, CORES), HALVES), lax.rem(slab, CORES)
    near_me, far_me = line * CORES + core, half * tiles + tile

    def near_peer(d):
        peer = shifted(near_me, d, near)
        return {"slab": lax.div(peer, CORES) * block + half * CORES + lax.rem(peer, CORES)}

    def far_peer(d):
        peer = shifted(far_me, d, far)
        return {"slab": line * block + lax.div(peer, tiles) * CORES + core, "tile": lax.rem(peer, tiles)}

    loads = [
        pltpu.make_async_copy(vel_hbm, flow.at[0, :, 1 : count + 1], load_sem.at[0]),
        pltpu.make_async_copy(nu_hbm, nu, load_sem.at[1]),
    ]
    for copy in loads:
        copy.start()

    barrier = pltpu.get_barrier_semaphore()
    greeted = [{"slab": shifted(slab, 1, slabs)}, {"slab": shifted(slab, -1, slabs)}]
    for d in range(1, near):
        greeted.append(near_peer(d))
    for d in range(1, far):
        greeted.append(far_peer(d))
    for device in greeted:
        pl.semaphore_signal(barrier, inc=1, device_id=device, device_id_type=MESH)

    def mode_copy(plane):
        return pltpu.make_async_copy(modes_hbm.at[:, plane], modes.at[:, plane], mode_sem.at[plane])

    for copy in loads:
        copy.wait()
    for plane in range(planes):
        mode_copy(plane).start()

    def edges(x, carry):
        for c in range(3):
            low_edge[0, c, pl.ds(x, 1)] = flow[0, c, x + 1, 0, 0:1]
            high_edge[0, c, pl.ds(x, 1)] = flow[0, c, x + 1, 1, SUB - 1 : SUB]
        return carry

    lax.fori_loop(0, count, edges, 0)
    pl.semaphore_wait(barrier, len(greeted))

    def faces(step):
        up_x, down_x = {"slab": shifted(slab, 1, slabs)}, {"slab": shifted(slab, -1, slabs)}
        up_z, down_z = {"tile": shifted(tile, 1, tiles)}, {"tile": shifted(tile, -1, tiles)}
        moves = [
            (low_edge.at[step], high.at[step], down_z),
            (high_edge.at[step], low.at[step], up_z),
            (flow.at[step, :, count], flow.at[step, :, 0], up_x),
            (flow.at[step, :, 1], flow.at[step, :, count + 1], down_x),
        ]
        return [
            pltpu.make_async_remote_copy(
                src_ref=source,
                dst_ref=target,
                send_sem=face_send.at[step, i],
                recv_sem=face_recv.at[step, i],
                device_id=device,
                device_id_type=MESH,
            )
            for i, (source, target, device) in enumerate(moves)
        ]

    def strip(k, owner):
        start = owner * width
        if k == 2:
            return advanced.at[:, pl.ds(start, width)]
        return flow.at[k, :, pl.ds(start + 1, width)]

    def bulk(k, d):
        owner = shifted(tile, d, tiles)
        return pltpu.make_async_remote_copy(
            src_ref=strip(k, owner),
            dst_ref=snaps.at[k, :, :, pl.ds(2 * tile, 2)],
            send_sem=bulk_send.at[k, d],
            recv_sem=bulk_recv.at[k, d],
            device_id={"tile": owner},
            device_id_type=MESH,
        )

    def own(k):
        return pltpu.make_async_copy(strip(k, tile), snaps.at[k, :, :, pl.ds(2 * tile, 2)], own_sem.at[k])

    def send_strips(k):
        for d in range(1, tiles):
            bulk(k, d).start()
        own(k).start()

    def gram_planes(first, last):
        def plane_step(plane, carry):
            mode_copy(plane).wait()
            columns = jnp.concatenate(
                [wide_pair(modes, plane, t) for t in range(0, modes.shape[2], 2)], axis=1
            )
            products[...] += lax.dot_general(
                columns, columns, (((1,), (1,)), ((), ())), preferred_element_type=F32
            )
            return carry

        lax.fori_loop(first, last, plane_step, 0)

    def reduce_start(size, me, peer_of, sums, send, recv):
        copies = [
            pltpu.make_async_remote_copy(
                src_ref=sums.at[0],
                dst_ref=sums.at[1 + me],
                send_sem=send.at[d],
                recv_sem=recv.at[d],
                device_id=peer_of(d),
                device_id_type=MESH,
            )
            for d in range(1, size)
        ]
        for copy in copies:
            copy.start()
        return copies

    def reduce_end(size, me, sums, copies):
        sums[1 + me] = sums[0]
        for copy in copies:
            copy.wait()
        total = sums[1]
        for i in range(1, size):
            total = total + sums[1 + i]
        return total

    def near_start(which, sums):
        return reduce_start(near, near_me, near_peer, sums, one_send.at[which], one_recv.at[which])

    def far_start(which, sums):
        return reduce_start(far, far_me, far_peer, sums, two_send.at[which], two_recv.at[which])

    first_faces = faces(0)
    for copy in first_faces:
        copy.start()
    send_strips(0)
    weight_row[...] = jnp.zeros_like(weight_row)
    weight_row[:, :RANK] = sigma_ref[...]
    products[...] = jnp.zeros_like(products)
    squares[...] = jnp.zeros_like(squares)
    gram_planes(0, planes)
    for copy in first_faces:
        copy.wait()

    def store_first(c, x, value):
        flow[1, c, x + 1] = value.reshape(2, SUB, LANES)
        low_edge[1, c, pl.ds(x, 1)] = value[0:1]
        high_edge[1, c, pl.ds(x, 1)] = value[2 * SUB - 1 :]

    advance_planes(flow.at[0], low.at[0], high.at[0], nu, store_first)
    second_faces = faces(1)
    for copy in second_faces:
        copy.start()
    send_strips(1)
    sums_one[0] = matched(products[...], RANK)
    basis_near = near_start(0, sums_one)
    for copy in second_faces:
        copy.wait()

    def store_second(c, x, value):
        advanced[c, x] = value.reshape(2, SUB, LANES)

    advance_planes(flow.at[1], low.at[1], high.at[1], nu, store_second)
    sums_two[0] = reduce_end(near, near_me, sums_one, basis_near)
    basis_far = far_start(0, sums_two)
    send_strips(2)
    snap_rows = 3 * SNAPS * SUB
    products[:snap_rows] = jnp.zeros((snap_rows, WIDE), F32)

    def gram_pieces(group):
        def piece(turn, carry):
            @pl.when(turn == 0)
            def _():
                for k in group:
                    own(k).wait()

            @pl.when(turn > 0)
            def _():
                for k in group:
                    bulk(k, turn).wait_recv()

            at = 2 * shifted(tile, -turn, tiles)
            columns = jnp.concatenate([wide_pair(modes, p, at) for p in range(planes)], axis=1)
            rows = []
            for k in group:
                flat = jnp.concatenate(
                    [
                        snaps[k, p // width, p % width, at + h]
                        for p in range(planes)
                        for h in range(2)
                    ],
                    axis=1,
                )
                rows.extend(pieces(flat, 3))
            first, last = 3 * SUB * group[0], 3 * SUB * (group[-1] + 1)
            products[first:last] += lax.dot_general(
                jnp.concatenate(rows, axis=0),
                columns,
                (((1,), (1,)), ((), ())),
                preferred_element_type=F32,
            )
            for a in group:
                for b in range(a + 1):
                    total = jnp.zeros((SUB, LANES), F32)
                    for p in range(planes):
                        for h in range(2):
                            c, w = divmod(p, width)
                            total = total + snaps[a, c, w, at + h] * snaps[b, c, w, at + h]
                    squares[3 * a + b] += total
            return carry

        lax.fori_loop(0, tiles, piece, 0)

    gram_pieces((0, 1))
    gram_pieces((2,))
    by_part = matched(products[:snap_rows], 3 * SNAPS)
    row = iota((SUB, LANES), 0)
    lane = iota((SUB, LANES), 1)
    result = jnp.zeros((SUB, LANES), F32)
    for s in range(SNAPS):
        at = 3 * s
        joined = by_part[at : at + 1] + by_part[at + 1 : at + 2] + by_part[at + 2 : at + 3]
        result = jnp.where(row == s, joined, result)
    for a in range(SNAPS):
        for b in range(a + 1):
            here = ((row == a) & (lane == RANK + b)) | ((row == b) & (lane == RANK + a))
            result = jnp.where(here, jnp.sum(squares[3 * a + b]), result)
    late_sums_one[0] = result
    late_near = near_start(1, late_sums_one)
    weight = weight_row[...]
    early_row = iota((RANK, LANES), 0)
    early_lane = iota((RANK, LANES), 1)
    tall_weight = jnp.broadcast_to(weight, (LANES, LANES)).T[:RANK]
    early = reduce_end(far, far_me, sums_two, basis_far) * weight * tall_weight
    early = early + (early_lane == early_row + 64).astype(F32)
    blocks = [early[SUB * b : SUB * b + SUB] for b in range(RANK // SUB)]

    def eliminate(first, last):
        for i in range(first, last):
            at, inner = divmod(i, SUB)
            pivot_row = blocks[at][inner : inner + 1]
            scaled = pivot_row / pivot_row[:, i : i + 1]
            for b in range(at, RANK // SUB):
                update = blocks[b][:, i : i + 1] * scaled
                if b == at:
                    update = jnp.where(row > inner, update, 0.0)
                blocks[b] = blocks[b] - update

    eliminate(0, RANK // 2)
    late_sums_two[0] = reduce_end(near, near_me, late_sums_one, late_near)
    late_far = far_start(1, late_sums_two)
    eliminate(RANK // 2, RANK)
    eliminated = jnp.concatenate(blocks, axis=0)
    pivots = jnp.sum(jnp.where(early_lane == early_row, eliminated, 0.0), axis=1, keepdims=True)
    eliminated = eliminated / jnp.sqrt(pivots)
    early_ref[...] = jnp.where((early_lane >= early_row) | (early_lane >= 64), eliminated, 0.0)
    late_ref[...] = reduce_end(far, far_me, late_sums_two, late_far)

    for k in range(SNAPS):
        for d in range(1, tiles):
            bulk(k, d).wait_send()


def mix(row_scale, early_ref, late_ref, sigma_row, rotation_ref, factor_ref, weight_ref, snap_ref):
    row = iota((GRAM_ROWS, LANES), 0)
    lane = iota((GRAM_ROWS, LANES), 1)
    sub = iota((SUB, LANES), 0)
    short = iota((SUB, LANES), 1)
    top = early_ref[...]
    inverse_top = jnp.where(lane[:RANK] >= 64, top, 0.0)
    late = late_ref[...] * jnp.where(short < RANK, sigma_row, 1.0)
    cross = pltpu.roll(jnp.where(short < RANK, late, 0.0), 64, 1)
    placed = jnp.concatenate(
        [jnp.zeros((RANK, LANES), F32), cross, jnp.zeros((LANES - GRAM_ROWS, LANES), F32)], axis=0
    )
    lanes_both = (((1,), (1,)), ((), ()))
    top = top + lax.dot_general(
        inverse_top, placed, lanes_both, precision=HIGHEST, preferred_element_type=F32
    )
    weights = lax.dot_general(
        cross, inverse_top, lanes_both, precision=HIGHEST, preferred_element_type=F32
    )
    bottom = jnp.where(sub < SNAPS, late, 0.0) + (
        (short == sub + 64 + RANK) | ((short == sub + RANK) & (sub >= SNAPS))
    ).astype(F32)
    bottom = bottom - jnp.dot(weights, top, precision=HIGHEST, preferred_element_type=F32)
    for i in range(SNAPS):
        pivot_row = bottom[i : i + 1]
        scaled = pivot_row / pivot_row[:, RANK + i : RANK + i + 1]
        update = bottom[:, RANK + i : RANK + i + 1] * scaled
        bottom = bottom - jnp.where(sub > i, update, 0.0)
    pivots = jnp.sum(jnp.where(short == sub + RANK, bottom, 0.0), axis=1, keepdims=True)
    done = jnp.concatenate([top, bottom / jnp.sqrt(pivots)], axis=0)
    factor = jnp.where(lane >= row, done, 0.0) * (1.0 / row_scale)
    factor_ref[...] = factor[:K, :K]
    inverse = jnp.where(row < K, done, 0.0)
    mixed = row_scale * jnp.dot(
        rotation_ref[:, :GRAM_ROWS], inverse, precision=HIGHEST, preferred_element_type=F32
    )
    sigma_lane = pltpu.roll(sigma_row, 64, 1)
    spread = ((iota((LANES, WIDE), 0) - 64) == iota((LANES, WIDE), 1) // SUB).astype(BF16)
    same = iota((WIDE, WIDE), 0) % SUB == iota((WIDE, WIDE), 1) % SUB
    for part, values in enumerate(pieces(mixed * sigma_lane, 2)):
        wide = jnp.dot(values, spread, preferred_element_type=F32)
        tall = jnp.broadcast_to(wide[:, None, :], (RANK, SUB, WIDE)).reshape(WIDE, WIDE)
        weight_ref[WIDE * part : WIDE * part + WIDE] = jnp.where(same, tall, 0.0).astype(BF16)
    for s in range(SNAPS):
        column = mixed[:, 64 + RANK + s : 64 + RANK + s + 1]
        snap_ref[s] = jnp.broadcast_to(column[:, :, None], (RANK, SUB, LANES))


def rotate_kernel(
    row_scale,
    early_ref,
    late_ref,
    sigma_ref,
    rotation_ref,
    modes_hbm,
    snaps,
    flow,
    advanced,
    factor_ref,
    new_modes,
    modes,
    sigma_row,
    rotation_wide,
    weight_ref,
    snap_ref,
    staged,
    flow_sem,
    out_sem,
    mode_sem,
):
    planes, tiles = modes.shape[1], modes.shape[2]

    def mode_copy(plane):
        return pltpu.make_async_copy(modes_hbm.at[:, plane], modes.at[:, plane], mode_sem.at[plane])

    for plane in range(planes):
        mode_copy(plane).start()
    passing = pltpu.make_async_copy(flow, advanced, flow_sem)
    passing.start()
    sigma_row[...] = jnp.zeros_like(sigma_row)
    sigma_row[:, :RANK] = sigma_ref[...]
    rotation_wide[...] = jnp.zeros_like(rotation_wide)
    rotation_wide[:, :K] = rotation_ref[...]
    mix(
        row_scale, early_ref, late_ref, sigma_row[...], rotation_wide, factor_ref, weight_ref, snap_ref
    )
    width = snaps.shape[2]

    def out_copy(plane, slot):
        return pltpu.make_async_copy(staged.at[slot], new_modes.at[:, plane], out_sem.at[slot])

    def plane_step(plane, carry):
        slot = lax.rem(plane, 2)

        @pl.when(plane >= 2)
        def _():
            out_copy(plane - 2, slot).wait()

        mode_copy(plane).wait()
        c, w = lax.div(plane, width), lax.rem(plane, width)
        for t in range(0, tiles, 2):
            both = jnp.dot(weight_ref[...], wide_pair(modes, plane, t), preferred_element_type=F32)
            both = both[:WIDE] + both[WIDE:]
            for half in range(2):
                value = both[:, LANES * half : LANES * half + LANES].reshape(RANK, SUB, LANES)
                for s in range(SNAPS):
                    value = value + snap_ref[s] * snaps[s, c, w, t + half][None]
                staged[slot, :, t + half] = value.astype(BF16)
        out_copy(plane, slot).start()
        return carry

    lax.fori_loop(0, planes, plane_step, 0)
    for plane in (planes - 2, planes - 1):
        out_copy(plane, plane % 2).wait()
    passing.wait()


def hbm_spec():
    return pl.BlockSpec(memory_space=pltpu.HBM)


def vmem_spec():
    return pl.BlockSpec(memory_space=pltpu.VMEM)


def shards(slabs, tiles, velocity, viscosity, basis, sigma, rotation):
    _, parts, width, deep, lanes = basis.shape
    planes, deep_tiles = parts * width, deep // SUB
    count = velocity.shape[1]
    row_scale = math.sqrt(planes * deep * lanes * slabs * tiles)
    modes_hbm = basis.reshape(RANK, planes, deep_tiles, SUB, LANES)
    flow_shape = (3, count, 2, SUB, LANES)
    sigma_row = sigma.reshape(1, RANK)
    flow, early, late, snaps = pl.pallas_call(
        functools.partial(exchange_kernel, slabs, tiles),
        in_specs=[hbm_spec(), hbm_spec(), hbm_spec(), vmem_spec()],
        out_specs=[vmem_spec()] * 4,
        out_shape=[
            pltpu.VMEM(flow_shape, F32),
            pltpu.VMEM((RANK, LANES), F32),
            pltpu.VMEM((SUB, LANES), F32),
            pltpu.VMEM((SNAPS, parts, width, deep_tiles, SUB, LANES), F32),
        ],
        scratch_shapes=[
            pltpu.VMEM(modes_hbm.shape, BF16),
            pltpu.VMEM((2, 3, count + 2, 2, SUB, LANES), F32),
            pltpu.VMEM((count, 2, SUB, LANES), F32),
            pltpu.VMEM((2, 3, count, LANES), F32),
            pltpu.VMEM((2, 3, count, LANES), F32),
            pltpu.VMEM((2, 3, count, LANES), F32),
            pltpu.VMEM((2, 3, count, LANES), F32),
            pltpu.VMEM((WIDE, WIDE), F32),
            pltpu.VMEM((9, SUB, LANES), F32),
            pltpu.VMEM((1 + slabs // HALVES, RANK, LANES), F32),
            pltpu.VMEM((1 + HALVES * tiles, RANK, LANES), F32),
            pltpu.VMEM((1 + slabs // HALVES, SUB, LANES), F32),
            pltpu.VMEM((1 + HALVES * tiles, SUB, LANES), F32),
            pltpu.VMEM((1, LANES), F32),
            pltpu.SemaphoreType.DMA((2,)),
            pltpu.SemaphoreType.DMA((planes,)),
            pltpu.SemaphoreType.DMA((SNAPS,)),
            pltpu.SemaphoreType.DMA((2, 4)),
            pltpu.SemaphoreType.DMA((2, 4)),
            pltpu.SemaphoreType.DMA((SNAPS, tiles)),
            pltpu.SemaphoreType.DMA((SNAPS, tiles)),
            pltpu.SemaphoreType.DMA((2, slabs // HALVES)),
            pltpu.SemaphoreType.DMA((2, slabs // HALVES)),
            pltpu.SemaphoreType.DMA((2, HALVES * tiles)),
            pltpu.SemaphoreType.DMA((2, HALVES * tiles)),
        ],
        compiler_params=pltpu.CompilerParams(
            collective_id=0, has_side_effects=True, vmem_limit_bytes=EXCHANGE_VMEM
        ),
        name="exchange",
    )(velocity.reshape(flow_shape), viscosity.reshape(count, 2, SUB, LANES), modes_hbm, sigma_row)
    advanced, factor, rotated = pl.pallas_call(
        functools.partial(rotate_kernel, row_scale),
        in_specs=[vmem_spec()] * 4 + [hbm_spec(), vmem_spec(), vmem_spec()],
        out_specs=[hbm_spec(), vmem_spec(), hbm_spec()],
        out_shape=[
            jax.ShapeDtypeStruct(flow_shape, F32),
            jax.ShapeDtypeStruct((K, K), F32),
            jax.ShapeDtypeStruct(modes_hbm.shape, BF16),
        ],
        scratch_shapes=[
            pltpu.VMEM(modes_hbm.shape, BF16),
            pltpu.VMEM((1, LANES), F32),
            pltpu.VMEM((RANK, LANES), F32),
            pltpu.VMEM((2 * WIDE, WIDE), BF16),
            pltpu.VMEM((SNAPS, RANK, SUB, LANES), F32),
            pltpu.VMEM((2, RANK, deep_tiles, SUB, LANES), BF16),
            pltpu.SemaphoreType.DMA,
            pltpu.SemaphoreType.DMA((2,)),
            pltpu.SemaphoreType.DMA((planes,)),
        ],
        compiler_params=pltpu.CompilerParams(vmem_limit_bytes=ROTATE_VMEM),
        name="rotate",
    )(early, late, sigma_row, rotation.T, modes_hbm, snaps, flow)
    return (advanced.reshape(velocity.shape), factor, rotated.reshape(basis.shape))


def solution(mesh):
    in_specs = (
        P(None, "slab", "tile", None),
        P("slab", "tile", None),
        P(None, None, ("slab", "tile"), None, None),
        P(),
        P(),
    )
    out_specs = (P(None, "slab", "tile", None), P(), P(None, None, ("slab", "tile"), None, None))
    return jax.shard_map(
        functools.partial(shards, mesh.shape["slab"], mesh.shape["tile"]),
        mesh=mesh,
        in_specs=in_specs,
        out_specs=out_specs,
        check_vma=False,
    )
```

```python
import functools
import math

import jax
import jax.numpy as jnp
from jax import lax
from jax.experimental import pallas as pl
from jax.experimental.pallas import tpu as pltpu
from jax.sharding import PartitionSpec as P

step_size = 0.25
RANK = 32
SNAPS = 3
K = RANK + SNAPS
SUB = 8
LANES = 128
WIDE = RANK * SUB
F32 = jnp.float32
BF16 = jnp.bfloat16
HIGHEST = lax.Precision.HIGHEST
MESH = pl.DeviceIdType.MESH
GRAM_ROWS = 40
CORES = 2
HALVES = 2
EXCHANGE_VMEM = 25_900_000
ROTATE_VMEM = 10_000_000


def iota(shape, dim):
    return lax.broadcasted_iota(jnp.int32, shape, dim)


def pieces(values, count):
    parts = []
    for _ in range(count):
        part = values.astype(BF16)
        parts.append(part)
        values = values - part.astype(F32)
    return parts


def matched(product, rows):
    same = iota(product.shape, 0) % SUB == iota(product.shape, 1) % SUB
    summed = jnp.where(same, product, 0.0).reshape(rows, SUB, WIDE).sum(1)
    pick = (iota((WIDE, LANES), 0) // SUB == iota((WIDE, LANES), 1)).astype(F32)
    return jnp.dot(summed, pick, precision=HIGHEST, preferred_element_type=F32)


def wide_pair(ref, *index):
    *front, tile = index
    left = ref[(slice(None), *front, tile)].reshape(WIDE, LANES)
    right = ref[(slice(None), *front, tile + 1)].reshape(WIDE, LANES)
    return jnp.concatenate([left, right], axis=1)


def spread_weights(values, rows, out_ref):
    tall_rows = rows * SUB
    spread = ((iota((LANES, WIDE), 0) - 64) == iota((LANES, WIDE), 1) // SUB).astype(BF16)
    same = iota((tall_rows, WIDE), 0) % SUB == iota((tall_rows, WIDE), 1) % SUB
    for part, piece in enumerate(pieces(values, 2)):
        wide = jnp.dot(piece, spread, preferred_element_type=F32)[:rows]
        tall = jnp.broadcast_to(wide[:, None, :], (rows, SUB, WIDE)).reshape(tall_rows, WIDE)
        out_ref[tall_rows * part : tall_rows * part + tall_rows] = jnp.where(same, tall, 0.0).astype(BF16)


def advance_planes(padded, low, high, viscosity, store):
    count = viscosity.shape[0]
    depth = 2 * SUB
    row = iota((depth, LANES), 0)
    lane = iota((depth, LANES), 1)

    def plane(x, carry):
        def at(c, p):
            return padded[c, p].reshape(depth, LANES)

        flow = [at(c, x + 1) for c in range(3)]
        nu = viscosity[x].reshape(depth, LANES)
        for c in range(3):
            centre = flow[c]
            forward_x, backward_x = at(c, x + 2), at(c, x)
            forward_z = jnp.where(row == depth - 1, high[c, pl.ds(x, 1)], pltpu.roll(centre, depth - 1, 0))
            backward_z = jnp.where(row == 0, low[c, pl.ds(x, 1)], pltpu.roll(centre, 1, 0))
            above_y = jnp.where(lane == LANES - 1, 0.0, pltpu.roll(centre, LANES - 1, 1))
            below_y = jnp.where(lane == 0, 0.0, pltpu.roll(centre, 1, 1))
            laplace = forward_x + backward_x + forward_z + backward_z + above_y + below_y - 6.0 * centre
            carried = (
                flow[0] * (forward_x - backward_x)
                + flow[1] * (above_y - below_y)
                + flow[2] * (forward_z - backward_z)
            )
            store(c, x, centre + step_size * (nu * laplace - 0.5 * carried))
        return carry

    lax.fori_loop(0, count, plane, 0)


def exchange_kernel(
    slabs,
    tiles,
    row_scale,
    vel_hbm,
    nu_hbm,
    modes_hbm,
    sigma_ref,
    rotation_ref,
    advanced,
    early_ref,
    late_ref,
    snaps,
    modes,
    partly,
    rotate_ref,
    rotation_wide,
    flow,
    nu,
    low,
    high,
    low_edge,
    high_edge,
    products,
    squares,
    sums_one,
    sums_two,
    late_sums_one,
    late_sums_two,
    weight_row,
    load_sem,
    mode_sem,
    own_sem,
    face_send,
    face_recv,
    bulk_send,
    bulk_recv,
    one_send,
    one_recv,
    two_send,
    two_recv,
):
    slab, tile = lax.axis_index("slab"), lax.axis_index("tile")
    planes = modes.shape[1]
    width = snaps.shape[2]
    count = nu.shape[0]

    def shifted(index, by, size):
        return lax.rem(index + by + size, size)

    block = HALVES * CORES
    near, far = slabs // HALVES, HALVES * tiles
    line, half, core = lax.div(slab, block), lax.rem(lax.div(slab, CORES), HALVES), lax.rem(slab, CORES)
    near_me, far_me = line * CORES + core, half * tiles + tile

    def near_peer(d):
        peer = shifted(near_me, d, near)
        return {"slab": lax.div(peer, CORES) * block + half * CORES + lax.rem(peer, CORES)}

    def far_peer(d):
        peer = shifted(far_me, d, far)
        return {"slab": line * block + lax.div(peer, tiles) * CORES + core, "tile": lax.rem(peer, tiles)}

    loads = [
        pltpu.make_async_copy(vel_hbm, flow.at[0, :, 1 : count + 1], load_sem.at[0]),
        pltpu.make_async_copy(nu_hbm, nu, load_sem.at[1]),
    ]
    for copy in loads:
        copy.start()

    barrier = pltpu.get_barrier_semaphore()
    greeted = [{"slab": shifted(slab, 1, slabs)}, {"slab": shifted(slab, -1, slabs)}]
    for d in range(1, near):
        greeted.append(near_peer(d))
    for d in range(1, far):
        greeted.append(far_peer(d))
    for device in greeted:
        pl.semaphore_signal(barrier, inc=1, device_id=device, device_id_type=MESH)

    def mode_copy(plane):
        return pltpu.make_async_copy(modes_hbm.at[:, plane], modes.at[:, plane], mode_sem.at[plane])

    for copy in loads:
        copy.wait()
    for plane in range(planes):
        mode_copy(plane).start()

    def edges(x, carry):
        for c in range(3):
            low_edge[0, c, pl.ds(x, 1)] = flow[0, c, x + 1, 0, 0:1]
            high_edge[0, c, pl.ds(x, 1)] = flow[0, c, x + 1, 1, SUB - 1 : SUB]
        return carry

    lax.fori_loop(0, count, edges, 0)
    pl.semaphore_wait(barrier, len(greeted))

    def faces(step):
        up_x, down_x = {"slab": shifted(slab, 1, slabs)}, {"slab": shifted(slab, -1, slabs)}
        up_z, down_z = {"tile": shifted(tile, 1, tiles)}, {"tile": shifted(tile, -1, tiles)}
        moves = [
            (low_edge.at[step], high.at[step], down_z),
            (high_edge.at[step], low.at[step], up_z),
            (flow.at[step, :, count], flow.at[step, :, 0], up_x),
            (flow.at[step, :, 1], flow.at[step, :, count + 1], down_x),
        ]
        return [
            pltpu.make_async_remote_copy(
                src_ref=source,
                dst_ref=target,
                send_sem=face_send.at[step, i],
                recv_sem=face_recv.at[step, i],
                device_id=device,
                device_id_type=MESH,
            )
            for i, (source, target, device) in enumerate(moves)
        ]

    def strip(k, owner):
        start = owner * width
        if k == 2:
            return advanced.at[:, pl.ds(start, width)]
        return flow.at[k, :, pl.ds(start + 1, width)]

    def bulk(k, d):
        owner = shifted(tile, d, tiles)
        return pltpu.make_async_remote_copy(
            src_ref=strip(k, owner),
            dst_ref=snaps.at[k, :, :, pl.ds(2 * tile, 2)],
            send_sem=bulk_send.at[k, d],
            recv_sem=bulk_recv.at[k, d],
            device_id={"tile": owner},
            device_id_type=MESH,
        )

    def own(k):
        return pltpu.make_async_copy(strip(k, tile), snaps.at[k, :, :, pl.ds(2 * tile, 2)], own_sem.at[k])

    def send_strips(k):
        for d in range(1, tiles):
            bulk(k, d).start()
        own(k).start()

    def gram_planes(first, last):
        def plane_step(plane, carry):
            mode_copy(plane).wait()
            columns = jnp.concatenate(
                [wide_pair(modes, plane, t) for t in range(0, modes.shape[2], 2)], axis=1
            )
            products[...] += lax.dot_general(
                columns, columns, (((1,), (1,)), ((), ())), preferred_element_type=F32
            )
            return carry

        lax.fori_loop(first, last, plane_step, 0)

    def reduce_start(size, me, peer_of, sums, send, recv):
        copies = [
            pltpu.make_async_remote_copy(
                src_ref=sums.at[0],
                dst_ref=sums.at[1 + me],
                send_sem=send.at[d],
                recv_sem=recv.at[d],
                device_id=peer_of(d),
                device_id_type=MESH,
            )
            for d in range(1, size)
        ]
        for copy in copies:
            copy.start()
        return copies

    def reduce_end(size, me, sums, copies):
        sums[1 + me] = sums[0]
        sent.extend(copies)
        for copy in copies:
            copy.wait_recv()
        total = sums[1]
        for i in range(1, size):
            total = total + sums[1 + i]
        return total

    def near_start(which, sums):
        return reduce_start(near, near_me, near_peer, sums, one_send.at[which], one_recv.at[which])

    def far_start(which, sums):
        return reduce_start(far, far_me, far_peer, sums, two_send.at[which], two_recv.at[which])

    sent = []
    first_faces = faces(0)
    for copy in first_faces:
        copy.start()
    send_strips(0)
    weight_row[...] = jnp.zeros_like(weight_row)
    weight_row[:, :RANK] = sigma_ref[...]
    products[...] = jnp.zeros_like(products)
    squares[...] = jnp.zeros_like(squares)
    gram_planes(0, planes)
    sent.extend(first_faces)
    for copy in first_faces:
        copy.wait_recv()

    def store_first(c, x, value):
        flow[1, c, x + 1] = value.reshape(2, SUB, LANES)
        low_edge[1, c, pl.ds(x, 1)] = value[0:1]
        high_edge[1, c, pl.ds(x, 1)] = value[2 * SUB - 1 :]

    advance_planes(flow.at[0], low.at[0], high.at[0], nu, store_first)
    second_faces = faces(1)
    for copy in second_faces:
        copy.start()
    send_strips(1)
    sums_one[0] = matched(products[...], RANK)
    basis_near = near_start(0, sums_one)
    sent.extend(second_faces)
    for copy in second_faces:
        copy.wait_recv()

    def store_second(c, x, value):
        advanced[c, x] = value.reshape(2, SUB, LANES)

    advance_planes(flow.at[1], low.at[1], high.at[1], nu, store_second)
    sums_two[0] = reduce_end(near, near_me, sums_one, basis_near)
    basis_far = far_start(0, sums_two)
    send_strips(2)
    snap_rows = 3 * SNAPS * SUB
    products[:snap_rows] = jnp.zeros((snap_rows, WIDE), F32)

    def gram_pieces(group):
        def piece(turn, carry):
            @pl.when(turn == 0)
            def _():
                for k in group:
                    own(k).wait()

            @pl.when(turn > 0)
            def _():
                for k in group:
                    bulk(k, turn).wait_recv()

            at = 2 * shifted(tile, -turn, tiles)
            columns = jnp.concatenate([wide_pair(modes, p, at) for p in range(planes)], axis=1)
            rows = []
            for k in group:
                flat = jnp.concatenate(
                    [
                        snaps[k, p // width, p % width, at + h]
                        for p in range(planes)
                        for h in range(2)
                    ],
                    axis=1,
                )
                rows.extend(pieces(flat, 3))
            first, last = 3 * SUB * group[0], 3 * SUB * (group[-1] + 1)
            products[first:last] += lax.dot_general(
                jnp.concatenate(rows, axis=0),
                columns,
                (((1,), (1,)), ((), ())),
                preferred_element_type=F32,
            )
            for a in group:
                for b in range(a + 1):
                    total = jnp.zeros((SUB, LANES), F32)
                    for p in range(planes):
                        for h in range(2):
                            c, w = divmod(p, width)
                            total = total + snaps[a, c, w, at + h] * snaps[b, c, w, at + h]
                    squares[3 * a + b] += total
            return carry

        lax.fori_loop(0, tiles, piece, 0)

    row = iota((SUB, LANES), 0)
    weight = weight_row[...]
    early_row = iota((RANK, LANES), 0)
    early_lane = iota((RANK, LANES), 1)
    tall_weight = jnp.broadcast_to(weight, (LANES, LANES)).T[:RANK]
    early = reduce_end(far, far_me, sums_two, basis_far) * weight * tall_weight
    early = early + (early_lane == early_row + 64).astype(F32)
    blocks = [early[SUB * b : SUB * b + SUB] for b in range(RANK // SUB)]

    def eliminate(first, last):
        for i in range(first, last):
            at, inner = divmod(i, SUB)
            pivot_row = blocks[at][inner : inner + 1]
            scaled = pivot_row / pivot_row[:, i : i + 1]
            for b in range(at, RANK // SUB):
                update = blocks[b][:, i : i + 1] * scaled
                if b == at:
                    update = jnp.where(row > inner, update, 0.0)
                blocks[b] = blocks[b] - update

    eliminate(0, RANK)
    eliminated = jnp.concatenate(blocks, axis=0)
    pivots = jnp.sum(jnp.where(early_lane == early_row, eliminated, 0.0), axis=1, keepdims=True)
    eliminated = eliminated / jnp.sqrt(pivots)
    early_ref[...] = jnp.where((early_lane >= early_row) | (early_lane >= 64), eliminated, 0.0)
    inverse_top = jnp.where(early_lane >= 64, eliminated, 0.0)
    rotation_wide[...] = jnp.zeros_like(rotation_wide)
    rotation_wide[:, :K] = rotation_ref[...]
    mixed = row_scale * jnp.dot(
        rotation_wide[:, :RANK], inverse_top, precision=HIGHEST, preferred_element_type=F32
    )
    spread_weights(mixed * pltpu.roll(weight, 64, 1), RANK, rotate_ref)

    def rotate_planes(first, last):
        def plane_step(plane, carry):
            for t in range(0, modes.shape[2], 2):
                both = jnp.dot(
                    rotate_ref[...], wide_pair(modes, plane, t), preferred_element_type=F32
                )
                both = both[:WIDE] + both[WIDE:]
                for half in range(2):
                    part = both[:, LANES * half : LANES * half + LANES]
                    partly[plane, t + half] = part.reshape(RANK, SUB, LANES)
            return carry

        lax.fori_loop(first, last, plane_step, 0)

    gram_pieces((0, 1, 2))
    by_part = matched(products[:snap_rows], 3 * SNAPS)
    lane = iota((SUB, LANES), 1)
    result = jnp.zeros((SUB, LANES), F32)
    for s in range(SNAPS):
        at = 3 * s
        joined = by_part[at : at + 1] + by_part[at + 1 : at + 2] + by_part[at + 2 : at + 3]
        result = jnp.where(row == s, joined, result)
    for a in range(SNAPS):
        for b in range(a + 1):
            here = ((row == a) & (lane == RANK + b)) | ((row == b) & (lane == RANK + a))
            result = jnp.where(here, jnp.sum(squares[3 * a + b]), result)
    late_sums_one[0] = result
    late_near = near_start(1, late_sums_one)
    rotate_planes(0, planes // 2)
    late_sums_two[0] = reduce_end(near, near_me, late_sums_one, late_near)
    late_far = far_start(1, late_sums_two)
    rotate_planes(planes // 2, planes)
    late_ref[...] = reduce_end(far, far_me, late_sums_two, late_far)

    for copy in sent:
        copy.wait_send()
    for k in range(SNAPS):
        for d in range(1, tiles):
            bulk(k, d).wait_send()


def mix(row_scale, early_ref, late_ref, sigma_row, rotation_ref, factor_ref, weight_ref, snap_ref):
    row = iota((GRAM_ROWS, LANES), 0)
    lane = iota((GRAM_ROWS, LANES), 1)
    sub = iota((SUB, LANES), 0)
    short = iota((SUB, LANES), 1)
    top = early_ref[...]
    inverse_top = jnp.where(lane[:RANK] >= 64, top, 0.0)
    late = late_ref[...] * jnp.where(short < RANK, sigma_row, 1.0)
    cross = pltpu.roll(jnp.where(short < RANK, late, 0.0), 64, 1)
    placed = jnp.concatenate(
        [jnp.zeros((RANK, LANES), F32), cross, jnp.zeros((LANES - GRAM_ROWS, LANES), F32)], axis=0
    )
    lanes_both = (((1,), (1,)), ((), ()))
    top = top + lax.dot_general(
        inverse_top, placed, lanes_both, precision=HIGHEST, preferred_element_type=F32
    )
    weights = lax.dot_general(
        cross, inverse_top, lanes_both, precision=HIGHEST, preferred_element_type=F32
    )
    bottom = jnp.where(sub < SNAPS, late, 0.0) + (
        (short == sub + 64 + RANK) | ((short == sub + RANK) & (sub >= SNAPS))
    ).astype(F32)
    bottom = bottom - jnp.dot(weights, top, precision=HIGHEST, preferred_element_type=F32)
    for i in range(SNAPS):
        pivot_row = bottom[i : i + 1]
        scaled = pivot_row / pivot_row[:, RANK + i : RANK + i + 1]
        update = bottom[:, RANK + i : RANK + i + 1] * scaled
        bottom = bottom - jnp.where(sub > i, update, 0.0)
    pivots = jnp.sum(jnp.where(short == sub + RANK, bottom, 0.0), axis=1, keepdims=True)
    done = jnp.concatenate([top, bottom / jnp.sqrt(pivots)], axis=0)
    factor = jnp.where(lane >= row, done, 0.0) * (1.0 / row_scale)
    factor_ref[...] = factor[:K, :K]
    inverse = jnp.where(row < K, done, 0.0)
    mixed = row_scale * jnp.dot(
        rotation_ref[:, :GRAM_ROWS], inverse, precision=HIGHEST, preferred_element_type=F32
    )
    removed = jnp.dot(weights, inverse_top, precision=HIGHEST, preferred_element_type=F32)
    spread_weights(removed * pltpu.roll(sigma_row, 64, 1), SNAPS, weight_ref)
    for s in range(SNAPS):
        column = mixed[:, 64 + RANK + s : 64 + RANK + s + 1]
        snap_ref[s] = jnp.broadcast_to(column[:, :, None], (RANK, SUB, LANES))


def rotate_kernel(
    row_scale,
    early_ref,
    late_ref,
    sigma_ref,
    rotation_ref,
    modes,
    partly,
    snaps,
    flow,
    advanced,
    factor_ref,
    new_modes,
    sigma_row,
    rotation_wide,
    weight_ref,
    snap_ref,
    staged,
    flow_sem,
    out_sem,
):
    planes, tiles = modes.shape[1], modes.shape[2]

    passing = pltpu.make_async_copy(flow, advanced, flow_sem)
    passing.start()
    sigma_row[...] = jnp.zeros_like(sigma_row)
    sigma_row[:, :RANK] = sigma_ref[...]
    rotation_wide[...] = jnp.zeros_like(rotation_wide)
    rotation_wide[:, :K] = rotation_ref[...]
    mix(
        row_scale, early_ref, late_ref, sigma_row[...], rotation_wide, factor_ref, weight_ref, snap_ref
    )
    width = snaps.shape[2]

    def out_copy(plane, slot):
        return pltpu.make_async_copy(staged.at[slot], new_modes.at[:, plane], out_sem.at[slot])

    def plane_step(plane, carry):
        slot = lax.rem(plane, 2)

        @pl.when(plane >= 2)
        def _():
            out_copy(plane - 2, slot).wait()

        c, w = lax.div(plane, width), lax.rem(plane, width)
        for t in range(0, tiles, 2):
            both = jnp.dot(weight_ref[...], wide_pair(modes, plane, t), preferred_element_type=F32)
            both = both[: SNAPS * SUB] + both[SNAPS * SUB :]
            for half in range(2):
                value = partly[plane, t + half]
                for s in range(SNAPS):
                    inside = both[SUB * s : SUB * s + SUB, LANES * half : LANES * half + LANES]
                    value = value + snap_ref[s] * (snaps[s, c, w, t + half] - inside)[None]
                staged[slot, :, t + half] = value.astype(BF16)
        out_copy(plane, slot).start()
        return carry

    lax.fori_loop(0, planes, plane_step, 0)
    for plane in (planes - 2, planes - 1):
        out_copy(plane, plane % 2).wait()
    passing.wait()


def hbm_spec():
    return pl.BlockSpec(memory_space=pltpu.HBM)


def vmem_spec():
    return pl.BlockSpec(memory_space=pltpu.VMEM)


def shards(slabs, tiles, velocity, viscosity, basis, sigma, rotation):
    _, parts, width, deep, lanes = basis.shape
    planes, deep_tiles = parts * width, deep // SUB
    count = velocity.shape[1]
    row_scale = math.sqrt(planes * deep * lanes * slabs * tiles)
    modes_hbm = basis.reshape(RANK, planes, deep_tiles, SUB, LANES)
    flow_shape = (3, count, 2, SUB, LANES)
    sigma_row = sigma.reshape(1, RANK)
    flow, early, late, snaps, modes, partly = pl.pallas_call(
        functools.partial(exchange_kernel, slabs, tiles, row_scale),
        in_specs=[hbm_spec(), hbm_spec(), hbm_spec(), vmem_spec(), vmem_spec()],
        out_specs=[vmem_spec()] * 6,
        out_shape=[
            pltpu.VMEM(flow_shape, F32),
            pltpu.VMEM((RANK, LANES), F32),
            pltpu.VMEM((SUB, LANES), F32),
            pltpu.VMEM((SNAPS, parts, width, deep_tiles, SUB, LANES), F32),
            pltpu.VMEM(modes_hbm.shape, BF16),
            pltpu.VMEM((planes, deep_tiles, RANK, SUB, LANES), F32),
        ],
        scratch_shapes=[
            pltpu.VMEM((2 * WIDE, WIDE), BF16),
            pltpu.VMEM((RANK, LANES), F32),
            pltpu.VMEM((2, 3, count + 2, 2, SUB, LANES), F32),
            pltpu.VMEM((count, 2, SUB, LANES), F32),
            pltpu.VMEM((2, 3, count, LANES), F32),
            pltpu.VMEM((2, 3, count, LANES), F32),
            pltpu.VMEM((2, 3, count, LANES), F32),
            pltpu.VMEM((2, 3, count, LANES), F32),
            pltpu.VMEM((WIDE, WIDE), F32),
            pltpu.VMEM((9, SUB, LANES), F32),
            pltpu.VMEM((1 + slabs // HALVES, RANK, LANES), F32),
            pltpu.VMEM((1 + HALVES * tiles, RANK, LANES), F32),
            pltpu.VMEM((1 + slabs // HALVES, SUB, LANES), F32),
            pltpu.VMEM((1 + HALVES * tiles, SUB, LANES), F32),
            pltpu.VMEM((1, LANES), F32),
            pltpu.SemaphoreType.DMA((2,)),
            pltpu.SemaphoreType.DMA((planes,)),
            pltpu.SemaphoreType.DMA((SNAPS,)),
            pltpu.SemaphoreType.DMA((2, 4)),
            pltpu.SemaphoreType.DMA((2, 4)),
            pltpu.SemaphoreType.DMA((SNAPS, tiles)),
            pltpu.SemaphoreType.DMA((SNAPS, tiles)),
            pltpu.SemaphoreType.DMA((2, slabs // HALVES)),
            pltpu.SemaphoreType.DMA((2, slabs // HALVES)),
            pltpu.SemaphoreType.DMA((2, HALVES * tiles)),
            pltpu.SemaphoreType.DMA((2, HALVES * tiles)),
        ],
        compiler_params=pltpu.CompilerParams(
            collective_id=0, has_side_effects=True, vmem_limit_bytes=EXCHANGE_VMEM
        ),
        name="exchange",
    )(velocity.reshape(flow_shape), viscosity.reshape(count, 2, SUB, LANES), modes_hbm, sigma_row, rotation.T)
    advanced, factor, rotated = pl.pallas_call(
        functools.partial(rotate_kernel, row_scale),
        in_specs=[vmem_spec()] * 8,
        out_specs=[hbm_spec(), vmem_spec(), hbm_spec()],
        out_shape=[
            jax.ShapeDtypeStruct(flow_shape, F32),
            jax.ShapeDtypeStruct((K, K), F32),
            jax.ShapeDtypeStruct(modes_hbm.shape, BF16),
        ],
        scratch_shapes=[
            pltpu.VMEM((1, LANES), F32),
            pltpu.VMEM((RANK, LANES), F32),
            pltpu.VMEM((2 * SNAPS * SUB, WIDE), BF16),
            pltpu.VMEM((SNAPS, RANK, SUB, LANES), F32),
            pltpu.VMEM((2, RANK, deep_tiles, SUB, LANES), BF16),
            pltpu.SemaphoreType.DMA,
            pltpu.SemaphoreType.DMA((2,)),
        ],
        compiler_params=pltpu.CompilerParams(vmem_limit_bytes=ROTATE_VMEM),
        name="rotate",
    )(early, late, sigma_row, rotation.T, modes, partly, snaps, flow)
    return (advanced.reshape(velocity.shape), factor, rotated.reshape(basis.shape))


def solution(mesh):
    in_specs = (
        P(None, "slab", "tile", None),
        P("slab", "tile", None),
        P(None, None, ("slab", "tile"), None, None),
        P(),
        P(),
    )
    out_specs = (P(None, "slab", "tile", None), P(), P(None, None, ("slab", "tile"), None, None))
    return jax.shard_map(
        functools.partial(shards, mesh.shape["slab"], mesh.shape["tile"]),
        mesh=mesh,
        in_specs=in_specs,
        out_specs=out_specs,
        check_vma=False,
    )
```

```python
import functools
import math

import jax
import jax.numpy as jnp
from jax import lax
from jax.experimental import pallas as pl
from jax.experimental.pallas import tpu as pltpu
from jax.sharding import PartitionSpec as P

step_size = 0.25
RANK = 32
SNAPS = 3
K = RANK + SNAPS
SUB = 8
LANES = 128
WIDE = RANK * SUB
F32 = jnp.float32
BF16 = jnp.bfloat16
HIGHEST = lax.Precision.HIGHEST
MESH = pl.DeviceIdType.MESH
GRAM_ROWS = 40
CORES = 2
HALVES = 2
EXCHANGE_VMEM = 25_900_000
ROTATE_VMEM = 10_000_000


def iota(shape, dim):
    return lax.broadcasted_iota(jnp.int32, shape, dim)


def pieces(values, count):
    parts = []
    for _ in range(count):
        part = values.astype(BF16)
        parts.append(part)
        values = values - part.astype(F32)
    return parts


def matched(product, rows):
    same = iota(product.shape, 0) % SUB == iota(product.shape, 1) % SUB
    summed = jnp.where(same, product, 0.0).reshape(rows, SUB, WIDE).sum(1)
    pick = (iota((WIDE, LANES), 0) // SUB == iota((WIDE, LANES), 1)).astype(F32)
    return jnp.dot(summed, pick, precision=HIGHEST, preferred_element_type=F32)


def wide_pair(ref, *index):
    *front, tile = index
    left = ref[(slice(None), *front, tile)].reshape(WIDE, LANES)
    right = ref[(slice(None), *front, tile + 1)].reshape(WIDE, LANES)
    return jnp.concatenate([left, right], axis=1)


def spread_weights(values, rows, out_ref):
    tall_rows = rows * SUB
    spread = ((iota((LANES, WIDE), 0) - 64) == iota((LANES, WIDE), 1) // SUB).astype(BF16)
    same = iota((tall_rows, WIDE), 0) % SUB == iota((tall_rows, WIDE), 1) % SUB
    for part, piece in enumerate(pieces(values, 2)):
        wide = jnp.dot(piece, spread, preferred_element_type=F32)[:rows]
        tall = jnp.broadcast_to(wide[:, None, :], (rows, SUB, WIDE)).reshape(tall_rows, WIDE)
        out_ref[tall_rows * part : tall_rows * part + tall_rows] = jnp.where(same, tall, 0.0).astype(BF16)


def advance_planes(padded, low, high, viscosity, store):
    count = viscosity.shape[0]
    depth = 2 * SUB
    row = iota((depth, LANES), 0)
    lane = iota((depth, LANES), 1)

    def plane(x, carry):
        def at(c, p):
            return padded[c, p].reshape(depth, LANES)

        flow = [at(c, x + 1) for c in range(3)]
        nu = viscosity[x].reshape(depth, LANES)
        for c in range(3):
            centre = flow[c]
            forward_x, backward_x = at(c, x + 2), at(c, x)
            forward_z = jnp.where(row == depth - 1, high[c, pl.ds(x, 1)], pltpu.roll(centre, depth - 1, 0))
            backward_z = jnp.where(row == 0, low[c, pl.ds(x, 1)], pltpu.roll(centre, 1, 0))
            above_y = jnp.where(lane == LANES - 1, 0.0, pltpu.roll(centre, LANES - 1, 1))
            below_y = jnp.where(lane == 0, 0.0, pltpu.roll(centre, 1, 1))
            laplace = forward_x + backward_x + forward_z + backward_z + above_y + below_y - 6.0 * centre
            carried = (
                flow[0] * (forward_x - backward_x)
                + flow[1] * (above_y - below_y)
                + flow[2] * (forward_z - backward_z)
            )
            store(c, x, centre + step_size * (nu * laplace - 0.5 * carried))
        return carry

    lax.fori_loop(0, count, plane, 0)


def exchange_kernel(
    slabs,
    tiles,
    row_scale,
    vel_hbm,
    nu_hbm,
    modes_hbm,
    sigma_ref,
    rotation_ref,
    advanced,
    early_ref,
    late_ref,
    snaps,
    modes,
    partly,
    rotate_ref,
    rotation_wide,
    flow,
    nu,
    low,
    high,
    low_edge,
    high_edge,
    products,
    squares,
    sums_one,
    sums_two,
    late_sums_one,
    late_sums_two,
    weight_row,
    load_sem,
    mode_sem,
    own_sem,
    face_send,
    face_recv,
    bulk_send,
    bulk_recv,
    one_send,
    one_recv,
    two_send,
    two_recv,
):
    slab, tile = lax.axis_index("slab"), lax.axis_index("tile")
    planes = modes.shape[1]
    width = snaps.shape[2]
    count = nu.shape[0]

    def shifted(index, by, size):
        return lax.rem(index + by + size, size)

    block = HALVES * CORES
    near, far = slabs // HALVES, HALVES * tiles
    line, half, core = lax.div(slab, block), lax.rem(lax.div(slab, CORES), HALVES), lax.rem(slab, CORES)
    near_me, far_me = line * CORES + core, half * tiles + tile

    def near_peer(d):
        peer = shifted(near_me, d, near)
        return {"slab": lax.div(peer, CORES) * block + half * CORES + lax.rem(peer, CORES)}

    def far_peer(d):
        peer = shifted(far_me, d, far)
        return {"slab": line * block + lax.div(peer, tiles) * CORES + core, "tile": lax.rem(peer, tiles)}

    loads = [
        pltpu.make_async_copy(vel_hbm, flow.at[0, :, 1 : count + 1], load_sem.at[0]),
        pltpu.make_async_copy(nu_hbm, nu, load_sem.at[1]),
    ]
    for copy in loads:
        copy.start()

    barrier = pltpu.get_barrier_semaphore()
    greeted = [{"slab": shifted(slab, 1, slabs)}, {"slab": shifted(slab, -1, slabs)}]
    for d in range(1, near):
        greeted.append(near_peer(d))
    for d in range(1, far):
        greeted.append(far_peer(d))
    for device in greeted:
        pl.semaphore_signal(barrier, inc=1, device_id=device, device_id_type=MESH)

    def mode_copy(plane):
        return pltpu.make_async_copy(modes_hbm.at[:, plane], modes.at[:, plane], mode_sem.at[plane])

    for copy in loads:
        copy.wait()
    for plane in range(planes):
        mode_copy(plane).start()

    def edges(x, carry):
        for c in range(3):
            low_edge[0, c, pl.ds(x, 1)] = flow[0, c, x + 1, 0, 0:1]
            high_edge[0, c, pl.ds(x, 1)] = flow[0, c, x + 1, 1, SUB - 1 : SUB]
        return carry

    lax.fori_loop(0, count, edges, 0)
    pl.semaphore_wait(barrier, len(greeted))

    def faces(step):
        up_x, down_x = {"slab": shifted(slab, 1, slabs)}, {"slab": shifted(slab, -1, slabs)}
        up_z, down_z = {"tile": shifted(tile, 1, tiles)}, {"tile": shifted(tile, -1, tiles)}
        moves = [
            (low_edge.at[step], high.at[step], down_z),
            (high_edge.at[step], low.at[step], up_z),
            (flow.at[step, :, count], flow.at[step, :, 0], up_x),
            (flow.at[step, :, 1], flow.at[step, :, count + 1], down_x),
        ]
        return [
            pltpu.make_async_remote_copy(
                src_ref=source,
                dst_ref=target,
                send_sem=face_send.at[step, i],
                recv_sem=face_recv.at[step, i],
                device_id=device,
                device_id_type=MESH,
            )
            for i, (source, target, device) in enumerate(moves)
        ]

    def strip(k, owner):
        start = owner * width
        if k == 2:
            return advanced.at[:, pl.ds(start, width)]
        return flow.at[k, :, pl.ds(start + 1, width)]

    def bulk(k, d):
        owner = shifted(tile, d, tiles)
        return pltpu.make_async_remote_copy(
            src_ref=strip(k, owner),
            dst_ref=snaps.at[k, :, :, pl.ds(2 * tile, 2)],
            send_sem=bulk_send.at[k, d],
            recv_sem=bulk_recv.at[k, d],
            device_id={"tile": owner},
            device_id_type=MESH,
        )

    def own(k):
        return pltpu.make_async_copy(strip(k, tile), snaps.at[k, :, :, pl.ds(2 * tile, 2)], own_sem.at[k])

    def send_strips(k):
        for d in range(1, tiles):
            bulk(k, d).start()
        own(k).start()

    def gram_planes(first, last):
        def plane_step(plane, carry):
            mode_copy(plane).wait()
            columns = jnp.concatenate(
                [wide_pair(modes, plane, t) for t in range(0, modes.shape[2], 2)], axis=1
            )
            products[...] += lax.dot_general(
                columns, columns, (((1,), (1,)), ((), ())), preferred_element_type=F32
            )
            return carry

        lax.fori_loop(first, last, plane_step, 0)

    def reduce_start(size, me, peer_of, sums, send, recv):
        copies = [
            pltpu.make_async_remote_copy(
                src_ref=sums.at[0],
                dst_ref=sums.at[1 + me],
                send_sem=send.at[d],
                recv_sem=recv.at[d],
                device_id=peer_of(d),
                device_id_type=MESH,
            )
            for d in range(1, size)
        ]
        for copy in copies:
            copy.start()
        return copies

    def reduce_end(size, me, sums, copies):
        sums[1 + me] = sums[0]
        sent.extend(copies)
        for copy in copies:
            copy.wait_recv()
        total = sums[1]
        for i in range(1, size):
            total = total + sums[1 + i]
        return total

    def near_start(which, sums):
        return reduce_start(near, near_me, near_peer, sums, one_send.at[which], one_recv.at[which])

    def far_start(which, sums):
        return reduce_start(far, far_me, far_peer, sums, two_send.at[which], two_recv.at[which])

    sent = []
    first_faces = faces(0)
    for copy in first_faces:
        copy.start()
    send_strips(0)
    weight_row[...] = jnp.zeros_like(weight_row)
    weight_row[:, :RANK] = sigma_ref[...]
    products[...] = jnp.zeros_like(products)
    squares[...] = jnp.zeros_like(squares)
    gram_planes(0, planes)
    sent.extend(first_faces)
    for copy in first_faces:
        copy.wait_recv()

    def store_first(c, x, value):
        flow[1, c, x + 1] = value.reshape(2, SUB, LANES)
        low_edge[1, c, pl.ds(x, 1)] = value[0:1]
        high_edge[1, c, pl.ds(x, 1)] = value[2 * SUB - 1 :]

    advance_planes(flow.at[0], low.at[0], high.at[0], nu, store_first)
    second_faces = faces(1)
    for copy in second_faces:
        copy.start()
    send_strips(1)
    sums_one[0] = matched(products[...], RANK)
    basis_near = near_start(0, sums_one)
    sent.extend(second_faces)
    for copy in second_faces:
        copy.wait_recv()

    def store_second(c, x, value):
        advanced[c, x] = value.reshape(2, SUB, LANES)

    advance_planes(flow.at[1], low.at[1], high.at[1], nu, store_second)
    sums_two[0] = reduce_end(near, near_me, sums_one, basis_near)
    basis_far = far_start(0, sums_two)
    send_strips(2)
    snap_rows = 3 * SNAPS * SUB
    products[:snap_rows] = jnp.zeros((snap_rows, WIDE), F32)

    def gram_pieces(group):
        def piece(turn, carry):
            @pl.when(turn == 0)
            def _():
                for k in group:
                    own(k).wait()

            @pl.when(turn > 0)
            def _():
                for k in group:
                    bulk(k, turn).wait_recv()

            at = 2 * shifted(tile, -turn, tiles)
            columns = jnp.concatenate([wide_pair(modes, p, at) for p in range(planes)], axis=1)
            rows = []
            for k in group:
                flat = jnp.concatenate(
                    [
                        snaps[k, p // width, p % width, at + h]
                        for p in range(planes)
                        for h in range(2)
                    ],
                    axis=1,
                )
                rows.extend(pieces(flat, 3))
            first, last = 3 * SUB * group[0], 3 * SUB * (group[-1] + 1)
            products[first:last] += lax.dot_general(
                jnp.concatenate(rows, axis=0),
                columns,
                (((1,), (1,)), ((), ())),
                preferred_element_type=F32,
            )
            for a in group:
                for b in range(a + 1):
                    total = jnp.zeros((SUB, LANES), F32)
                    for p in range(planes):
                        for h in range(2):
                            c, w = divmod(p, width)
                            total = total + snaps[a, c, w, at + h] * snaps[b, c, w, at + h]
                    squares[3 * a + b] += total
            return carry

        lax.fori_loop(0, tiles, piece, 0)

    row = iota((SUB, LANES), 0)
    weight = weight_row[...]
    early_row = iota((RANK, LANES), 0)
    early_lane = iota((RANK, LANES), 1)
    tall_weight = jnp.broadcast_to(weight, (LANES, LANES)).T[:RANK]
    early = reduce_end(far, far_me, sums_two, basis_far) * weight * tall_weight
    early = early + (early_lane == early_row + 64).astype(F32)
    blocks = [early[SUB * b : SUB * b + SUB] for b in range(RANK // SUB)]

    def eliminate(first, last):
        for i in range(first, last):
            at, inner = divmod(i, SUB)
            pivot_row = blocks[at][inner : inner + 1]
            scaled = pivot_row / pivot_row[:, i : i + 1]
            for b in range(at, RANK // SUB):
                update = blocks[b][:, i : i + 1] * scaled
                if b == at:
                    update = jnp.where(row > inner, update, 0.0)
                blocks[b] = blocks[b] - update

    eliminate(0, RANK)
    eliminated = jnp.concatenate(blocks, axis=0)
    pivots = jnp.sum(jnp.where(early_lane == early_row, eliminated, 0.0), axis=1, keepdims=True)
    eliminated = eliminated / jnp.sqrt(pivots)
    early_ref[...] = jnp.where((early_lane >= early_row) | (early_lane >= 64), eliminated, 0.0)
    inverse_top = jnp.where(early_lane >= 64, eliminated, 0.0)
    rotation_wide[...] = jnp.zeros_like(rotation_wide)
    rotation_wide[:, :K] = rotation_ref[...]
    mixed = row_scale * jnp.dot(
        rotation_wide[:, :RANK], inverse_top, precision=HIGHEST, preferred_element_type=F32
    )
    spread_weights(mixed * pltpu.roll(weight, 64, 1), RANK, rotate_ref)

    def rotate_planes(first, last):
        def plane_step(plane, carry):
            for t in range(0, modes.shape[2], 2):
                both = jnp.dot(
                    rotate_ref[...], wide_pair(modes, plane, t), preferred_element_type=F32
                )
                both = both[:WIDE] + both[WIDE:]
                for half in range(2):
                    part = both[:, LANES * half : LANES * half + LANES]
                    partly[plane, t + half] = part.reshape(RANK, SUB, LANES)
            return carry

        lax.fori_loop(first, last, plane_step, 0)

    gram_pieces((0, 1, 2))
    by_part = matched(products[:snap_rows], 3 * SNAPS)
    lane = iota((SUB, LANES), 1)
    result = jnp.zeros((SUB, LANES), F32)
    for s in range(SNAPS):
        at = 3 * s
        joined = by_part[at : at + 1] + by_part[at + 1 : at + 2] + by_part[at + 2 : at + 3]
        result = jnp.where(row == s, joined, result)
    for a in range(SNAPS):
        for b in range(a + 1):
            here = ((row == a) & (lane == RANK + b)) | ((row == b) & (lane == RANK + a))
            result = jnp.where(here, jnp.sum(squares[3 * a + b]), result)
    late_sums_one[0] = result
    late_near = near_start(1, late_sums_one)
    rotate_planes(0, planes // 2)
    late_sums_two[0] = reduce_end(near, near_me, late_sums_one, late_near)
    late_far = far_start(1, late_sums_two)
    rotate_planes(planes // 2, planes)
    late_ref[...] = reduce_end(far, far_me, late_sums_two, late_far)

    for copy in sent:
        copy.wait_send()
    for k in range(SNAPS):
        for d in range(1, tiles):
            bulk(k, d).wait_send()


def mix(row_scale, early_ref, late_ref, sigma_row, rotation_ref, factor_ref, weight_ref, snap_ref):
    row = iota((GRAM_ROWS, LANES), 0)
    lane = iota((GRAM_ROWS, LANES), 1)
    sub = iota((SUB, LANES), 0)
    short = iota((SUB, LANES), 1)
    top = early_ref[...]
    inverse_top = jnp.where(lane[:RANK] >= 64, top, 0.0)
    late = late_ref[...] * jnp.where(short < RANK, sigma_row, 1.0)
    cross = pltpu.roll(jnp.where(short < RANK, late, 0.0), 64, 1)
    placed = jnp.concatenate(
        [jnp.zeros((RANK, LANES), F32), cross, jnp.zeros((LANES - GRAM_ROWS, LANES), F32)], axis=0
    )
    lanes_both = (((1,), (1,)), ((), ()))
    top = top + lax.dot_general(
        inverse_top, placed, lanes_both, precision=HIGHEST, preferred_element_type=F32
    )
    weights = lax.dot_general(
        cross, inverse_top, lanes_both, precision=HIGHEST, preferred_element_type=F32
    )
    bottom = jnp.where(sub < SNAPS, late, 0.0) + (
        (short == sub + 64 + RANK) | ((short == sub + RANK) & (sub >= SNAPS))
    ).astype(F32)
    bottom = bottom - jnp.dot(weights, top, precision=HIGHEST, preferred_element_type=F32)
    for i in range(SNAPS):
        pivot_row = bottom[i : i + 1]
        scaled = pivot_row / pivot_row[:, RANK + i : RANK + i + 1]
        update = bottom[:, RANK + i : RANK + i + 1] * scaled
        bottom = bottom - jnp.where(sub > i, update, 0.0)
    pivots = jnp.sum(jnp.where(short == sub + RANK, bottom, 0.0), axis=1, keepdims=True)
    done = jnp.concatenate([top, bottom / jnp.sqrt(pivots)], axis=0)
    factor = jnp.where(lane >= row, done, 0.0) * (1.0 / row_scale)
    factor_ref[...] = factor[:K, :K]
    inverse = jnp.where(row < K, done, 0.0)
    mixed = row_scale * jnp.dot(
        rotation_ref[:, :GRAM_ROWS], inverse, precision=HIGHEST, preferred_element_type=F32
    )
    removed = jnp.dot(weights, inverse_top, precision=HIGHEST, preferred_element_type=F32)
    spread_weights(removed * pltpu.roll(sigma_row, 64, 1), SNAPS, weight_ref)
    column = iota((LANES, LANES), 1)
    picks = (iota((LANES, LANES), 0) - 64 - RANK) == lax.rem(column, SNAPS * SUB) // SUB
    high_part, low_part = pieces(mixed, 2)
    first = (picks & (column < 2 * SNAPS * SUB)).astype(BF16)
    second = (picks & (column >= 2 * SNAPS * SUB) & (column < 3 * SNAPS * SUB)).astype(BF16)
    wide = jnp.dot(high_part, first, preferred_element_type=F32)
    wide = wide + jnp.dot(low_part, second, preferred_element_type=F32)
    tall = jnp.broadcast_to(wide[:, None, :], (RANK, SUB, LANES)).reshape(WIDE, LANES)
    same = iota((WIDE, LANES), 0) % SUB == iota((WIDE, LANES), 1) % SUB
    snap_ref[...] = jnp.where(same, tall, 0.0).astype(BF16)


def rotate_kernel(
    row_scale,
    early_ref,
    late_ref,
    sigma_ref,
    rotation_ref,
    modes,
    partly,
    snaps,
    flow,
    advanced,
    factor_ref,
    new_modes,
    sigma_row,
    rotation_wide,
    weight_ref,
    snap_ref,
    staged,
    flow_sem,
    out_sem,
):
    planes, tiles = modes.shape[1], modes.shape[2]

    passing = pltpu.make_async_copy(flow, advanced, flow_sem)
    passing.start()
    sigma_row[...] = jnp.zeros_like(sigma_row)
    sigma_row[:, :RANK] = sigma_ref[...]
    rotation_wide[...] = jnp.zeros_like(rotation_wide)
    rotation_wide[:, :K] = rotation_ref[...]
    mix(
        row_scale, early_ref, late_ref, sigma_row[...], rotation_wide, factor_ref, weight_ref, snap_ref
    )
    width = snaps.shape[2]

    def out_copy(plane, slot):
        return pltpu.make_async_copy(staged.at[slot], new_modes.at[:, plane], out_sem.at[slot])

    def plane_step(plane, carry):
        slot = lax.rem(plane, 2)

        @pl.when(plane >= 2)
        def _():
            out_copy(plane - 2, slot).wait()

        c, w = lax.div(plane, width), lax.rem(plane, width)
        for t in range(0, tiles, 2):
            both = jnp.dot(weight_ref[...], wide_pair(modes, plane, t), preferred_element_type=F32)
            both = both[: SNAPS * SUB] + both[SNAPS * SUB :]
            flows = [
                jnp.concatenate([snaps[s, c, w, t], snaps[s, c, w, t + 1]], axis=1)
                for s in range(SNAPS)
            ]
            rest = jnp.concatenate(flows, axis=0) - both
            coarse = rest.astype(BF16).astype(F32)
            empty = jnp.zeros((LANES - 3 * SNAPS * SUB, 2 * LANES), F32)
            stack = jnp.concatenate([coarse, rest - coarse, coarse, empty], axis=0).astype(BF16)
            added = jnp.dot(snap_ref[...], stack, preferred_element_type=F32)
            for half in range(2):
                part = added[:, LANES * half : LANES * half + LANES].reshape(RANK, SUB, LANES)
                staged[slot, :, t + half] = (partly[plane, t + half] + part).astype(BF16)
        out_copy(plane, slot).start()
        return carry

    lax.fori_loop(0, planes, plane_step, 0)
    for plane in (planes - 2, planes - 1):
        out_copy(plane, plane % 2).wait()
    passing.wait()


def hbm_spec():
    return pl.BlockSpec(memory_space=pltpu.HBM)


def vmem_spec():
    return pl.BlockSpec(memory_space=pltpu.VMEM)


def shards(slabs, tiles, velocity, viscosity, basis, sigma, rotation):
    _, parts, width, deep, lanes = basis.shape
    planes, deep_tiles = parts * width, deep // SUB
    count = velocity.shape[1]
    row_scale = math.sqrt(planes * deep * lanes * slabs * tiles)
    modes_hbm = basis.reshape(RANK, planes, deep_tiles, SUB, LANES)
    flow_shape = (3, count, 2, SUB, LANES)
    sigma_row = sigma.reshape(1, RANK)
    flow, early, late, snaps, modes, partly = pl.pallas_call(
        functools.partial(exchange_kernel, slabs, tiles, row_scale),
        in_specs=[hbm_spec(), hbm_spec(), hbm_spec(), vmem_spec(), vmem_spec()],
        out_specs=[vmem_spec()] * 6,
        out_shape=[
            pltpu.VMEM(flow_shape, F32),
            pltpu.VMEM((RANK, LANES), F32),
            pltpu.VMEM((SUB, LANES), F32),
            pltpu.VMEM((SNAPS, parts, width, deep_tiles, SUB, LANES), F32),
            pltpu.VMEM(modes_hbm.shape, BF16),
            pltpu.VMEM((planes, deep_tiles, RANK, SUB, LANES), F32),
        ],
        scratch_shapes=[
            pltpu.VMEM((2 * WIDE, WIDE), BF16),
            pltpu.VMEM((RANK, LANES), F32),
            pltpu.VMEM((2, 3, count + 2, 2, SUB, LANES), F32),
            pltpu.VMEM((count, 2, SUB, LANES), F32),
            pltpu.VMEM((2, 3, count, LANES), F32),
            pltpu.VMEM((2, 3, count, LANES), F32),
            pltpu.VMEM((2, 3, count, LANES), F32),
            pltpu.VMEM((2, 3, count, LANES), F32),
            pltpu.VMEM((WIDE, WIDE), F32),
            pltpu.VMEM((9, SUB, LANES), F32),
            pltpu.VMEM((1 + slabs // HALVES, RANK, LANES), F32),
            pltpu.VMEM((1 + HALVES * tiles, RANK, LANES), F32),
            pltpu.VMEM((1 + slabs // HALVES, SUB, LANES), F32),
            pltpu.VMEM((1 + HALVES * tiles, SUB, LANES), F32),
            pltpu.VMEM((1, LANES), F32),
            pltpu.SemaphoreType.DMA((2,)),
            pltpu.SemaphoreType.DMA((planes,)),
            pltpu.SemaphoreType.DMA((SNAPS,)),
            pltpu.SemaphoreType.DMA((2, 4)),
            pltpu.SemaphoreType.DMA((2, 4)),
            pltpu.SemaphoreType.DMA((SNAPS, tiles)),
            pltpu.SemaphoreType.DMA((SNAPS, tiles)),
            pltpu.SemaphoreType.DMA((2, slabs // HALVES)),
            pltpu.SemaphoreType.DMA((2, slabs // HALVES)),
            pltpu.SemaphoreType.DMA((2, HALVES * tiles)),
            pltpu.SemaphoreType.DMA((2, HALVES * tiles)),
        ],
        compiler_params=pltpu.CompilerParams(
            collective_id=0, has_side_effects=True, vmem_limit_bytes=EXCHANGE_VMEM
        ),
        name="exchange",
    )(velocity.reshape(flow_shape), viscosity.reshape(count, 2, SUB, LANES), modes_hbm, sigma_row, rotation.T)
    advanced, factor, rotated = pl.pallas_call(
        functools.partial(rotate_kernel, row_scale),
        in_specs=[vmem_spec()] * 8,
        out_specs=[hbm_spec(), vmem_spec(), hbm_spec()],
        out_shape=[
            jax.ShapeDtypeStruct(flow_shape, F32),
            jax.ShapeDtypeStruct((K, K), F32),
            jax.ShapeDtypeStruct(modes_hbm.shape, BF16),
        ],
        scratch_shapes=[
            pltpu.VMEM((1, LANES), F32),
            pltpu.VMEM((RANK, LANES), F32),
            pltpu.VMEM((2 * SNAPS * SUB, WIDE), BF16),
            pltpu.VMEM((WIDE, LANES), BF16),
            pltpu.VMEM((2, RANK, deep_tiles, SUB, LANES), BF16),
            pltpu.SemaphoreType.DMA,
            pltpu.SemaphoreType.DMA((2,)),
        ],
        compiler_params=pltpu.CompilerParams(vmem_limit_bytes=ROTATE_VMEM),
        name="rotate",
    )(early, late, sigma_row, rotation.T, modes, partly, snaps, flow)
    return (advanced.reshape(velocity.shape), factor, rotated.reshape(basis.shape))


def solution(mesh):
    in_specs = (
        P(None, "slab", "tile", None),
        P("slab", "tile", None),
        P(None, None, ("slab", "tile"), None, None),
        P(),
        P(),
    )
    out_specs = (P(None, "slab", "tile", None), P(), P(None, None, ("slab", "tile"), None, None))
    return jax.shard_map(
        functools.partial(shards, mesh.shape["slab"], mesh.shape["tile"]),
        mesh=mesh,
        in_specs=in_specs,
        out_specs=out_specs,
        check_vma=False,
    )
```

```python
import functools
import math

import jax
import jax.numpy as jnp
from jax import lax
from jax.experimental import pallas as pl
from jax.experimental.pallas import tpu as pltpu
from jax.sharding import PartitionSpec as P

step_size = 0.25
RANK = 32
SNAPS = 3
K = RANK + SNAPS
SUB = 8
LANES = 128
WIDE = RANK * SUB
F32 = jnp.float32
BF16 = jnp.bfloat16
HIGHEST = lax.Precision.HIGHEST
MESH = pl.DeviceIdType.MESH
GRAM_ROWS = 40
CORES = 2
HALVES = 2
EXCHANGE_VMEM = 63_700_000
ROTATE_VMEM = 50 << 20


def iota(shape, dim):
    return lax.broadcasted_iota(jnp.int32, shape, dim)


def pieces(values, count):
    parts = []
    for _ in range(count):
        part = values.astype(BF16)
        parts.append(part)
        values = values - part.astype(F32)
    return parts


def matched(product, rows):
    same = iota(product.shape, 0) % SUB == iota(product.shape, 1) % SUB
    summed = jnp.where(same, product, 0.0).reshape(rows, SUB, WIDE).sum(1)
    pick = (iota((WIDE, LANES), 0) // SUB == iota((WIDE, LANES), 1)).astype(F32)
    return jnp.dot(summed, pick, precision=HIGHEST, preferred_element_type=F32)


def wide_pair(ref, *index):
    *front, tile = index
    left = ref[(slice(None), *front, tile)].reshape(WIDE, LANES)
    right = ref[(slice(None), *front, tile + 1)].reshape(WIDE, LANES)
    return jnp.concatenate([left, right], axis=1)


def advance_planes(padded, low, high, viscosity, store):
    count = viscosity.shape[0]
    depth = 2 * SUB
    row = iota((depth, LANES), 0)
    lane = iota((depth, LANES), 1)

    def plane(x, carry):
        def at(c, p):
            return padded[c, p].reshape(depth, LANES)

        flow = [at(c, x + 1) for c in range(3)]
        nu = viscosity[x].reshape(depth, LANES)
        for c in range(3):
            centre = flow[c]
            forward_x, backward_x = at(c, x + 2), at(c, x)
            forward_z = jnp.where(row == depth - 1, high[c, pl.ds(x, 1)], pltpu.roll(centre, depth - 1, 0))
            backward_z = jnp.where(row == 0, low[c, pl.ds(x, 1)], pltpu.roll(centre, 1, 0))
            above_y = jnp.where(lane == LANES - 1, 0.0, pltpu.roll(centre, LANES - 1, 1))
            below_y = jnp.where(lane == 0, 0.0, pltpu.roll(centre, 1, 1))
            laplace = forward_x + backward_x + forward_z + backward_z + above_y + below_y - 6.0 * centre
            carried = (
                flow[0] * (forward_x - backward_x)
                + flow[1] * (above_y - below_y)
                + flow[2] * (forward_z - backward_z)
            )
            store(c, x, centre + step_size * (nu * laplace - 0.5 * carried))
        return carry

    lax.fori_loop(0, count, plane, 0)


def exchange_kernel(
    slabs,
    tiles,
    vel_hbm,
    nu_hbm,
    modes_hbm,
    sigma_ref,
    advanced,
    early_ref,
    late_ref,
    snaps,
    modes,
    flow,
    nu,
    low,
    high,
    low_edge,
    high_edge,
    products,
    squares,
    sums_one,
    sums_two,
    late_sums_one,
    late_sums_two,
    weight_row,
    load_sem,
    mode_sem,
    own_sem,
    face_send,
    face_recv,
    bulk_send,
    bulk_recv,
    one_send,
    one_recv,
    two_send,
    two_recv,
):
    slab, tile = lax.axis_index("slab"), lax.axis_index("tile")
    planes = modes.shape[1]
    width = snaps.shape[2]
    count = nu.shape[0]

    def shifted(index, by, size):
        return lax.rem(index + by + size, size)

    block = HALVES * CORES
    near, far = slabs // HALVES, HALVES * tiles
    line, half, core = lax.div(slab, block), lax.rem(lax.div(slab, CORES), HALVES), lax.rem(slab, CORES)
    near_me, far_me = line * CORES + core, half * tiles + tile

    def near_peer(d):
        peer = shifted(near_me, d, near)
        return {"slab": lax.div(peer, CORES) * block + half * CORES + lax.rem(peer, CORES)}

    def far_peer(d):
        peer = shifted(far_me, d, far)
        return {"slab": line * block + lax.div(peer, tiles) * CORES + core, "tile": lax.rem(peer, tiles)}

    loads = [
        pltpu.make_async_copy(vel_hbm, flow.at[0, :, 1 : count + 1], load_sem.at[0]),
        pltpu.make_async_copy(nu_hbm, nu, load_sem.at[1]),
    ]
    for copy in loads:
        copy.start()

    barrier = pltpu.get_barrier_semaphore()
    greeted = [{"slab": shifted(slab, 1, slabs)}, {"slab": shifted(slab, -1, slabs)}]
    for d in range(1, near):
        greeted.append(near_peer(d))
    for d in range(1, far):
        greeted.append(far_peer(d))
    for device in greeted:
        pl.semaphore_signal(barrier, inc=1, device_id=device, device_id_type=MESH)

    def mode_copy(plane):
        return pltpu.make_async_copy(modes_hbm.at[:, plane], modes.at[:, plane], mode_sem.at[plane])

    for copy in loads:
        copy.wait()
    for plane in range(planes):
        mode_copy(plane).start()

    def edges(x, carry):
        for c in range(3):
            low_edge[0, c, pl.ds(x, 1)] = flow[0, c, x + 1, 0, 0:1]
            high_edge[0, c, pl.ds(x, 1)] = flow[0, c, x + 1, 1, SUB - 1 : SUB]
        return carry

    lax.fori_loop(0, count, edges, 0)
    pl.semaphore_wait(barrier, len(greeted))

    def faces(step):
        up_x, down_x = {"slab": shifted(slab, 1, slabs)}, {"slab": shifted(slab, -1, slabs)}
        up_z, down_z = {"tile": shifted(tile, 1, tiles)}, {"tile": shifted(tile, -1, tiles)}
        moves = [
            (low_edge.at[step], high.at[step], down_z),
            (high_edge.at[step], low.at[step], up_z),
            (flow.at[step, :, count], flow.at[step, :, 0], up_x),
            (flow.at[step, :, 1], flow.at[step, :, count + 1], down_x),
        ]
        return [
            pltpu.make_async_remote_copy(
                src_ref=source,
                dst_ref=target,
                send_sem=face_send.at[step, i],
                recv_sem=face_recv.at[step, i],
                device_id=device,
                device_id_type=MESH,
            )
            for i, (source, target, device) in enumerate(moves)
        ]

    def strip(k, owner):
        start = owner * width
        if k == 2:
            return advanced.at[:, pl.ds(start, width)]
        return flow.at[k, :, pl.ds(start + 1, width)]

    def bulk(k, d):
        owner = shifted(tile, d, tiles)
        return pltpu.make_async_remote_copy(
            src_ref=strip(k, owner),
            dst_ref=snaps.at[k, :, :, pl.ds(2 * tile, 2)],
            send_sem=bulk_send.at[k, d],
            recv_sem=bulk_recv.at[k, d],
            device_id={"tile": owner},
            device_id_type=MESH,
        )

    def own(k):
        return pltpu.make_async_copy(strip(k, tile), snaps.at[k, :, :, pl.ds(2 * tile, 2)], own_sem.at[k])

    def send_strips(k):
        for d in range(1, tiles):
            bulk(k, d).start()
        own(k).start()

    def gram_planes(first, last):
        def plane_step(plane, carry):
            mode_copy(plane).wait()
            columns = jnp.concatenate(
                [wide_pair(modes, plane, t) for t in range(0, modes.shape[2], 2)], axis=1
            )
            products[...] += lax.dot_general(
                columns, columns, (((1,), (1,)), ((), ())), preferred_element_type=F32
            )
            return carry

        lax.fori_loop(first, last, plane_step, 0)

    def reduce_start(size, me, peer_of, sums, send, recv):
        copies = [
            pltpu.make_async_remote_copy(
                src_ref=sums.at[0],
                dst_ref=sums.at[1 + me],
                send_sem=send.at[d],
                recv_sem=recv.at[d],
                device_id=peer_of(d),
                device_id_type=MESH,
            )
            for d in range(1, size)
        ]
        for copy in copies:
            copy.start()
        return copies

    def reduce_end(size, me, sums, copies):
        sums[1 + me] = sums[0]
        sent.extend(copies)
        for copy in copies:
            copy.wait_recv()
        total = sums[1]
        for i in range(1, size):
            total = total + sums[1 + i]
        return total

    def near_start(which, sums):
        return reduce_start(near, near_me, near_peer, sums, one_send.at[which], one_recv.at[which])

    def far_start(which, sums):
        return reduce_start(far, far_me, far_peer, sums, two_send.at[which], two_recv.at[which])

    sent = []
    first_faces = faces(0)
    for copy in first_faces:
        copy.start()
    send_strips(0)
    weight_row[...] = jnp.zeros_like(weight_row)
    weight_row[:, :RANK] = sigma_ref[...]
    products[...] = jnp.zeros_like(products)
    squares[...] = jnp.zeros_like(squares)
    gram_planes(0, planes)
    sent.extend(first_faces)
    for copy in first_faces:
        copy.wait_recv()

    def store_first(c, x, value):
        flow[1, c, x + 1] = value.reshape(2, SUB, LANES)
        low_edge[1, c, pl.ds(x, 1)] = value[0:1]
        high_edge[1, c, pl.ds(x, 1)] = value[2 * SUB - 1 :]

    advance_planes(flow.at[0], low.at[0], high.at[0], nu, store_first)
    second_faces = faces(1)
    for copy in second_faces:
        copy.start()
    send_strips(1)
    sums_one[0] = matched(products[...], RANK)
    basis_near = near_start(0, sums_one)
    sent.extend(second_faces)
    for copy in second_faces:
        copy.wait_recv()

    def store_second(c, x, value):
        advanced[c, x] = value.reshape(2, SUB, LANES)

    advance_planes(flow.at[1], low.at[1], high.at[1], nu, store_second)
    sums_two[0] = reduce_end(near, near_me, sums_one, basis_near)
    basis_far = far_start(0, sums_two)
    send_strips(2)
    snap_rows = 3 * SNAPS * SUB
    products[:snap_rows] = jnp.zeros((snap_rows, WIDE), F32)

    def gram_pieces(group):
        def piece(turn, carry):
            @pl.when(turn == 0)
            def _():
                for k in group:
                    own(k).wait()

            @pl.when(turn > 0)
            def _():
                for k in group:
                    bulk(k, turn).wait_recv()

            at = 2 * shifted(tile, -turn, tiles)
            columns = jnp.concatenate([wide_pair(modes, p, at) for p in range(planes)], axis=1)
            rows = []
            for k in group:
                flat = jnp.concatenate(
                    [
                        snaps[k, p // width, p % width, at + h]
                        for p in range(planes)
                        for h in range(2)
                    ],
                    axis=1,
                )
                rows.extend(pieces(flat, 3))
            first, last = 3 * SUB * group[0], 3 * SUB * (group[-1] + 1)
            products[first:last] += lax.dot_general(
                jnp.concatenate(rows, axis=0),
                columns,
                (((1,), (1,)), ((), ())),
                preferred_element_type=F32,
            )
            for a in group:
                for b in range(a + 1):
                    total = jnp.zeros((SUB, LANES), F32)
                    for p in range(planes):
                        for h in range(2):
                            c, w = divmod(p, width)
                            total = total + snaps[a, c, w, at + h] * snaps[b, c, w, at + h]
                    squares[3 * a + b] += total
            return carry

        lax.fori_loop(0, tiles, piece, 0)

    row = iota((SUB, LANES), 0)
    weight = weight_row[...]
    early_row = iota((RANK, LANES), 0)
    early_lane = iota((RANK, LANES), 1)
    tall_weight = jnp.broadcast_to(weight, (LANES, LANES)).T[:RANK]
    early = reduce_end(far, far_me, sums_two, basis_far) * weight * tall_weight
    early = early + (early_lane == early_row + 64).astype(F32)
    blocks = [early[SUB * b : SUB * b + SUB] for b in range(RANK // SUB)]

    def eliminate(first, last):
        for i in range(first, last):
            at, inner = divmod(i, SUB)
            pivot_row = blocks[at][inner : inner + 1]
            scaled = pivot_row / pivot_row[:, i : i + 1]
            for b in range(at, RANK // SUB):
                update = blocks[b][:, i : i + 1] * scaled
                if b == at:
                    update = jnp.where(row > inner, update, 0.0)
                blocks[b] = blocks[b] - update

    eliminate(0, RANK)
    gram_pieces((0, 1, 2))
    by_part = matched(products[:snap_rows], 3 * SNAPS)
    row = iota((SUB, LANES), 0)
    lane = iota((SUB, LANES), 1)
    result = jnp.zeros((SUB, LANES), F32)
    for s in range(SNAPS):
        at = 3 * s
        joined = by_part[at : at + 1] + by_part[at + 1 : at + 2] + by_part[at + 2 : at + 3]
        result = jnp.where(row == s, joined, result)
    for a in range(SNAPS):
        for b in range(a + 1):
            here = ((row == a) & (lane == RANK + b)) | ((row == b) & (lane == RANK + a))
            result = jnp.where(here, jnp.sum(squares[3 * a + b]), result)
    late_sums_one[0] = result
    late_near = near_start(1, late_sums_one)
    late_sums_two[0] = reduce_end(near, near_me, late_sums_one, late_near)
    late_far = far_start(1, late_sums_two)
    eliminated = jnp.concatenate(blocks, axis=0)
    pivots = jnp.sum(jnp.where(early_lane == early_row, eliminated, 0.0), axis=1, keepdims=True)
    eliminated = eliminated / jnp.sqrt(pivots)
    early_ref[...] = jnp.where((early_lane >= early_row) | (early_lane >= 64), eliminated, 0.0)
    late_ref[...] = reduce_end(far, far_me, late_sums_two, late_far)

    for copy in sent:
        copy.wait_send()
    for k in range(SNAPS):
        for d in range(1, tiles):
            bulk(k, d).wait_send()


def mix(row_scale, early_ref, late_ref, sigma_row, rotation_ref, factor_ref, weight_ref, snap_ref):
    row = iota((GRAM_ROWS, LANES), 0)
    lane = iota((GRAM_ROWS, LANES), 1)
    sub = iota((SUB, LANES), 0)
    short = iota((SUB, LANES), 1)
    top = early_ref[...]
    inverse_top = jnp.where(lane[:RANK] >= 64, top, 0.0)
    late = late_ref[...] * jnp.where(short < RANK, sigma_row, 1.0)
    cross = pltpu.roll(jnp.where(short < RANK, late, 0.0), 64, 1)
    placed = jnp.concatenate(
        [jnp.zeros((RANK, LANES), F32), cross, jnp.zeros((LANES - GRAM_ROWS, LANES), F32)], axis=0
    )
    lanes_both = (((1,), (1,)), ((), ()))
    top = top + lax.dot_general(
        inverse_top, placed, lanes_both, precision=HIGHEST, preferred_element_type=F32
    )
    weights = lax.dot_general(
        cross, inverse_top, lanes_both, precision=HIGHEST, preferred_element_type=F32
    )
    bottom = jnp.where(sub < SNAPS, late, 0.0) + (
        (short == sub + 64 + RANK) | ((short == sub + RANK) & (sub >= SNAPS))
    ).astype(F32)
    bottom = bottom - jnp.dot(weights, top, precision=HIGHEST, preferred_element_type=F32)
    for i in range(SNAPS):
        pivot_row = bottom[i : i + 1]
        scaled = pivot_row / pivot_row[:, RANK + i : RANK + i + 1]
        update = bottom[:, RANK + i : RANK + i + 1] * scaled
        bottom = bottom - jnp.where(sub > i, update, 0.0)
    pivots = jnp.sum(jnp.where(short == sub + RANK, bottom, 0.0), axis=1, keepdims=True)
    done = jnp.concatenate([top, bottom / jnp.sqrt(pivots)], axis=0)
    factor = jnp.where(lane >= row, done, 0.0) * (1.0 / row_scale)
    factor_ref[...] = factor[:K, :K]
    inverse = jnp.where(row < K, done, 0.0)
    mixed = row_scale * jnp.dot(
        rotation_ref[:, :GRAM_ROWS], inverse, precision=HIGHEST, preferred_element_type=F32
    )
    sigma_lane = pltpu.roll(sigma_row, 64, 1)
    spread = ((iota((LANES, WIDE), 0) - 64) == iota((LANES, WIDE), 1) // SUB).astype(BF16)
    same = iota((WIDE, WIDE), 0) % SUB == iota((WIDE, WIDE), 1) % SUB
    for part, values in enumerate(pieces(mixed * sigma_lane, 2)):
        wide = jnp.dot(values, spread, preferred_element_type=F32)
        tall = jnp.broadcast_to(wide[:, None, :], (RANK, SUB, WIDE)).reshape(WIDE, WIDE)
        weight_ref[WIDE * part : WIDE * part + WIDE] = jnp.where(same, tall, 0.0).astype(BF16)
    for s in range(SNAPS):
        column = mixed[:, 64 + RANK + s : 64 + RANK + s + 1]
        snap_ref[s] = jnp.broadcast_to(column[:, :, None], (RANK, SUB, LANES))


def rotate_kernel(
    row_scale,
    early_ref,
    late_ref,
    sigma_ref,
    rotation_ref,
    modes_hbm,
    snaps,
    flow,
    advanced,
    factor_ref,
    new_modes,
    modes,
    sigma_row,
    rotation_wide,
    weight_ref,
    snap_ref,
    staged,
    flow_sem,
    out_sem,
    mode_sem,
):
    planes, tiles = modes.shape[1], modes.shape[2]

    def mode_copy(plane):
        return pltpu.make_async_copy(modes_hbm.at[:, plane], modes.at[:, plane], mode_sem.at[plane])

    for plane in range(planes):
        mode_copy(plane).start()
    passing = pltpu.make_async_copy(flow, advanced, flow_sem)
    passing.start()
    sigma_row[...] = jnp.zeros_like(sigma_row)
    sigma_row[:, :RANK] = sigma_ref[...]
    rotation_wide[...] = jnp.zeros_like(rotation_wide)
    rotation_wide[:, :K] = rotation_ref[...]
    mix(
        row_scale, early_ref, late_ref, sigma_row[...], rotation_wide, factor_ref, weight_ref, snap_ref
    )
    width = snaps.shape[2]

    def out_copy(plane, slot):
        return pltpu.make_async_copy(staged.at[slot], new_modes.at[:, plane], out_sem.at[slot])

    def plane_step(plane, carry):
        slot = lax.rem(plane, 4)

        @pl.when(plane >= 4)
        def _():
            out_copy(plane - 4, slot).wait()

        mode_copy(plane).wait()
        c, w = lax.div(plane, width), lax.rem(plane, width)
        for t in range(0, tiles, 2):
            both = jnp.dot(weight_ref[...], wide_pair(modes, plane, t), preferred_element_type=F32)
            both = both[:WIDE] + both[WIDE:]
            for half in range(2):
                value = both[:, LANES * half : LANES * half + LANES].reshape(RANK, SUB, LANES)
                for s in range(SNAPS):
                    value = value + snap_ref[s] * snaps[s, c, w, t + half][None]
                staged[slot, :, t + half] = value.astype(BF16)
        out_copy(plane, slot).start()
        return carry

    lax.fori_loop(0, planes, plane_step, 0)
    for plane in range(planes - 4, planes):
        out_copy(plane, plane % 4).wait()
    passing.wait()


def hbm_spec():
    return pl.BlockSpec(memory_space=pltpu.HBM)


def vmem_spec():
    return pl.BlockSpec(memory_space=pltpu.VMEM)


def shards(slabs, tiles, velocity, viscosity, basis, sigma, rotation):
    _, parts, width, deep, lanes = basis.shape
    planes, deep_tiles = parts * width, deep // SUB
    count = velocity.shape[1]
    row_scale = math.sqrt(planes * deep * lanes * slabs * tiles)
    modes_hbm = basis.reshape(RANK, planes, deep_tiles, SUB, LANES)
    flow_shape = (3, count, 2, SUB, LANES)
    sigma_row = sigma.reshape(1, RANK)
    flow, early, late, snaps = pl.pallas_call(
        functools.partial(exchange_kernel, slabs, tiles),
        in_specs=[hbm_spec(), hbm_spec(), hbm_spec(), vmem_spec()],
        out_specs=[vmem_spec()] * 4,
        out_shape=[
            pltpu.VMEM(flow_shape, F32),
            pltpu.VMEM((RANK, LANES), F32),
            pltpu.VMEM((SUB, LANES), F32),
            pltpu.VMEM((SNAPS, parts, width, deep_tiles, SUB, LANES), F32),
        ],
        scratch_shapes=[
            pltpu.VMEM(modes_hbm.shape, BF16),
            pltpu.VMEM((2, 3, count + 2, 2, SUB, LANES), F32),
            pltpu.VMEM((count, 2, SUB, LANES), F32),
            pltpu.VMEM((2, 3, count, LANES), F32),
            pltpu.VMEM((2, 3, count, LANES), F32),
            pltpu.VMEM((2, 3, count, LANES), F32),
            pltpu.VMEM((2, 3, count, LANES), F32),
            pltpu.VMEM((WIDE, WIDE), F32),
            pltpu.VMEM((9, SUB, LANES), F32),
            pltpu.VMEM((1 + slabs // HALVES, RANK, LANES), F32),
            pltpu.VMEM((1 + HALVES * tiles, RANK, LANES), F32),
            pltpu.VMEM((1 + slabs // HALVES, SUB, LANES), F32),
            pltpu.VMEM((1 + HALVES * tiles, SUB, LANES), F32),
            pltpu.VMEM((1, LANES), F32),
            pltpu.SemaphoreType.DMA((2,)),
            pltpu.SemaphoreType.DMA((planes,)),
            pltpu.SemaphoreType.DMA((SNAPS,)),
            pltpu.SemaphoreType.DMA((2, 4)),
            pltpu.SemaphoreType.DMA((2, 4)),
            pltpu.SemaphoreType.DMA((SNAPS, tiles)),
            pltpu.SemaphoreType.DMA((SNAPS, tiles)),
            pltpu.SemaphoreType.DMA((2, slabs // HALVES)),
            pltpu.SemaphoreType.DMA((2, slabs // HALVES)),
            pltpu.SemaphoreType.DMA((2, HALVES * tiles)),
            pltpu.SemaphoreType.DMA((2, HALVES * tiles)),
        ],
        compiler_params=pltpu.CompilerParams(
            collective_id=0, has_side_effects=True, vmem_limit_bytes=EXCHANGE_VMEM
        ),
        name="exchange",
    )(velocity.reshape(flow_shape), viscosity.reshape(count, 2, SUB, LANES), modes_hbm, sigma_row)
    advanced, factor, rotated = pl.pallas_call(
        functools.partial(rotate_kernel, row_scale),
        in_specs=[vmem_spec()] * 4 + [hbm_spec(), vmem_spec(), vmem_spec()],
        out_specs=[hbm_spec(), vmem_spec(), hbm_spec()],
        out_shape=[
            jax.ShapeDtypeStruct(flow_shape, F32),
            jax.ShapeDtypeStruct((K, K), F32),
            jax.ShapeDtypeStruct(modes_hbm.shape, BF16),
        ],
        scratch_shapes=[
            pltpu.VMEM(modes_hbm.shape, BF16),
            pltpu.VMEM((1, LANES), F32),
            pltpu.VMEM((RANK, LANES), F32),
            pltpu.VMEM((2 * WIDE, WIDE), BF16),
            pltpu.VMEM((SNAPS, RANK, SUB, LANES), F32),
            pltpu.VMEM((4, RANK, deep_tiles, SUB, LANES), BF16),
            pltpu.SemaphoreType.DMA,
            pltpu.SemaphoreType.DMA((4,)),
            pltpu.SemaphoreType.DMA((planes,)),
        ],
        compiler_params=pltpu.CompilerParams(vmem_limit_bytes=ROTATE_VMEM),
        name="rotate",
    )(early, late, sigma_row, rotation.T, modes_hbm, snaps, flow)
    return (advanced.reshape(velocity.shape), factor, rotated.reshape(basis.shape))


def solution(mesh):
    in_specs = (
        P(None, "slab", "tile", None),
        P("slab", "tile", None),
        P(None, None, ("slab", "tile"), None, None),
        P(),
        P(),
    )
    out_specs = (P(None, "slab", "tile", None), P(), P(None, None, ("slab", "tile"), None, None))
    return jax.shard_map(
        functools.partial(shards, mesh.shape["slab"], mesh.shape["tile"]),
        mesh=mesh,
        in_specs=in_specs,
        out_specs=out_specs,
        check_vma=False,
    )
```
